256 devices in a mesh: gx: 8 (over x_hi, y), gy: 16 (over z, core), gz: 2 (over x_lo).
Axes of the slice: x: 4 (x_hi: 2, x_lo: 2; x = x_hi * 2 + x_lo), y: 4, z: 8, core: 2. Of those that a mesh axis runs over, the one named last changes fastest.
Arguments:
- flow_vector_lowres: float32 [3, 4, 512, 1024], P(None, 'gz', 'gy', 'gx'), may hold values from -3 to 3
- heat_anomaly_lowres: float32 [4, 512, 1024], P('gz', 'gy', 'gx'), may hold values from -6 to 6
- salt_content_anomaly: float32 [8, 2048, 1024], P('gz', ('gx', 'gy')), may hold values from -6 to 6
Outputs:
- updated_velocity: float32 [3, 4, 512, 1024], P(None, 'gz', 'gy', 'gx')
- temperature_new: float32 [4, 512, 1024], P('gz', 'gy', 'gx')
- salinity_new: float32 [8, 2048, 1024], P('gz', ('gx', 'gy'))
The draws below stay inside these ranges and needn't reach their ends.
All inputs are finite; a program needn't handle non-finite values.
Results may differ from the reference program's by a relative error of at most 0.00002.
Values sent between devices are 32-bit elements; how exact they have to be, the bound alone decides.
No kernel may reach another device: no remote copies, remote signals or barrier semaphores. Data moves between devices by JAX's collectives and lax.ppermute only.
A program may use at most 128 MiB of HBM per device.

```python
import jax
import jax.numpy as jnp
from jax import lax

LOWRES_DEPTHS = 4
LOWRES_SPAN_X = 512
LOWRES_SPAN_Y = 1024


def block_scale(stream_key, shape, cuts, least, high):
    loudness, own = 1.0, jax.random.fold_in(stream_key, 6)
    for position, shards_of in cuts:
        steps = jnp.exp(jax.random.uniform(jax.random.fold_in(own, position), (shards_of,), jnp.float32, least / len(cuts), high / len(cuts)))
        loudness = loudness * jnp.repeat(steps, shape[position] // shards_of).reshape([-1 if axis == position else 1 for axis in range(len(shape))])
    return loudness


def scatter_about(stream_key, shape, width, most, split=(), dtype=jnp.bfloat16):
    loudness = block_scale(stream_key, shape, split, -0.22, 0.18) if split else 1.0
    entries = jax.random.normal(stream_key, shape, jnp.float32) * width * loudness
    return jnp.minimum(jnp.maximum(entries, -most), most).astype(dtype)


def setup_inputs(seed: int = 0) -> dict:
    key_list = jax.random.split(jax.random.key(seed), 4)
    return {
        "flow_vector_lowres": scatter_about(key_list[0], (3, LOWRES_DEPTHS, LOWRES_SPAN_X, LOWRES_SPAN_Y), 0.5, 3.0, ((1, 2), (2, 16), (3, 8)), jnp.float32),
        "heat_anomaly_lowres": scatter_about(key_list[1], (LOWRES_DEPTHS, LOWRES_SPAN_X, LOWRES_SPAN_Y), 1.0, 6.0, ((0, 2), (1, 16), (2, 8)), jnp.float32),
        "salt_content_anomaly": scatter_about(key_list[2], (2 * LOWRES_DEPTHS, 2 * LOWRES_SPAN_Y, 2 * LOWRES_SPAN_X), 1.0, 6.0, ((0, 2), (1, 128)), jnp.float32),
    }


time_step = 0.1
viscosity = 0.2
heat_diffusion = 0.15
salt_diffusion = 0.05
expansion = 1.0
thermal_expansion_curve = 0.5
contraction = 0.8
even_weights = (-0.0390625, 0.2734375, 0.8203125, -0.0546875)
odd_weights = (-0.0546875, 0.8203125, 0.2734375, -0.0390625)


def refine(padded, along_dim):
    length = padded.shape[along_dim] - 4
    even_part = even_weights[0] * lax.slice_in_dim(padded, 0, length, axis=along_dim)
    odd_part = odd_weights[0] * lax.slice_in_dim(padded, 1, length + 1, axis=along_dim)
    for offset in range(1, 4):
        even_part = even_part + even_weights[offset] * lax.slice_in_dim(padded, offset, offset + length, axis=along_dim)
        odd_part = odd_part + odd_weights[offset] * lax.slice_in_dim(padded, offset + 1, offset + 1 + length, axis=along_dim)
    target = list(even_part.shape)
    target[along_dim] = 2 * length
    return jnp.stack([even_part, odd_part], axis=along_dim + 1).reshape(target)


def window(padded, target, along_dim, offset):
    leading = padded.ndim - 3
    starts = [0] * leading + [1, 1, 1]
    starts[leading + along_dim] = offset
    limits = [start_at + extent for start_at, extent in zip(starts, target)]
    return lax.slice(padded, starts, limits)


def tendency(field, padded, speeds, spacing, diffusion):
    advection = jnp.zeros(field.shape, jnp.float32)
    neighbours = jnp.zeros(field.shape, jnp.float32)
    for along_dim in range(3):
        below_cells = window(padded, field.shape, along_dim, 0)
        above_cells = window(padded, field.shape, along_dim, 2)
        advect_speed = speeds[along_dim]
        advection = advection + jnp.maximum(advect_speed, 0.0) * (field - below_cells) + jnp.minimum(advect_speed, 0.0) * (above_cells - field)
        neighbours = neighbours + below_cells + above_cells
    return diffusion * (neighbours - 6.0 * field) / (spacing * spacing) - advection / spacing


def coarse_rates(prognostic_variables, padded, buoyancy):
    diffusion = jnp.array([viscosity, viscosity, viscosity, heat_diffusion], jnp.float32).reshape(4, 1, 1, 1)
    coarse_tendency_rate = tendency(prognostic_variables, padded, (prognostic_variables[0], prognostic_variables[1], prognostic_variables[2]), 1.0, diffusion)
    return jnp.concatenate([coarse_tendency_rate[:1] + buoyancy[None], coarse_tendency_rate[1:]], axis=0)


def restrict(refined_field):
    level_count = refined_field.shape[0]
    row_count = refined_field.shape[1]
    col_count = refined_field.shape[2]
    grouped = refined_field.reshape(level_count // 2, 2, row_count // 2, 2, col_count // 2, 2)
    return 0.125 * jnp.sum(grouped, axis=(1, 3, 5))


def fine_rates(refined, salt_content_anomaly, salt_padded):
    salt_rate = tendency(salt_content_anomaly, salt_padded, (refined[0], refined[2], refined[1]), 0.5, salt_diffusion)
    buoyant = expansion * refined[3] * (1.0 + thermal_expansion_curve * refined[3]) - contraction * salt_content_anomaly
    return salt_rate, restrict(buoyant)


def heun_rates(prognostic_variables, salt_content_anomaly):
    turned = jnp.transpose(prognostic_variables, (0, 1, 3, 2))
    padded = jnp.pad(turned, ((0, 0), (2, 2), (2, 2), (2, 2)))
    refined = refine(refine(refine(padded, 1), 2), 3)
    salt_rate, coarse_buoyancy = fine_rates(refined, salt_content_anomaly, jnp.pad(salt_content_anomaly, 1))
    near_rim = jnp.pad(prognostic_variables, ((0, 0), (1, 1), (1, 1), (1, 1)))
    return coarse_rates(prognostic_variables, near_rim, jnp.transpose(coarse_buoyancy, (0, 2, 1))), salt_rate


def reference(flow_vector_lowres, heat_anomaly_lowres, salt_content_anomaly):
    prognostic_variables = jnp.concatenate([flow_vector_lowres, heat_anomaly_lowres[None]], axis=0)
    coarse_tendency_rate, salt_rate = heun_rates(prognostic_variables, salt_content_anomaly)
    fields_mid = prognostic_variables + time_step * coarse_tendency_rate
    salt_mid = salt_content_anomaly + time_step * salt_rate
    coarse_rate_mid, salt_rate_mid = heun_rates(fields_mid, salt_mid)
    fields_end = 0.5 * prognostic_variables + 0.5 * (fields_mid + time_step * coarse_rate_mid)
    salt_end = 0.5 * salt_content_anomaly + 0.5 * (salt_mid + time_step * salt_rate_mid)
    return fields_end[:3], fields_end[3], salt_end
```

```python
import jax
import jax.numpy as jnp
import numpy as np
from jax import lax
from jax.experimental import pallas as pl
from jax.experimental.pallas import tpu as pltpu
from jax.sharding import PartitionSpec as P

F32 = jnp.float32
BF16 = jnp.bfloat16
DT = 0.1
EVEN = (-0.0390625, 0.2734375, 0.8203125, -0.0546875)
ODD = (-0.0546875, 0.8203125, 0.2734375, -0.0390625)
KINDS = (0.2, 0.2, 0.2, 0.15)
NX = 512
NF = 1024


def refine_matrix():
    matrix = np.zeros((256, 256), np.float32)
    for n in range(256):
        i = 64 + n // 2
        for k in range(4):
            matrix[i + k - (2 if n % 2 == 0 else 1), n] = (EVEN if n % 2 == 0 else ODD)[k]
    return matrix


def restrict_matrix():
    matrix = np.zeros((256, 128), np.float32)
    for n in range(256):
        matrix[n, n // 2] = 0.125
    return matrix


REFINE = refine_matrix()
REFINE_SPLIT = np.concatenate([REFINE[:, 0::2], REFINE[:, 1::2]], axis=1)
RESTRICT = restrict_matrix()


def dot(a, b):
    return jnp.dot(a, b, preferred_element_type=F32)


def split(x):
    high = x.astype(BF16)
    return high, (x - high.astype(F32)).astype(BF16)


def row(x, s):
    n = x.shape[0]
    return x if s % n == 0 else pltpu.roll(x, (-s) % n, 0)


def iota(shape, axis):
    return lax.broadcasted_iota(jnp.int32, shape, axis)


def right(x):
    n = x.shape[1]
    return jnp.where(iota(x.shape, 1) == n - 1, 0.0, pltpu.roll(x, n - 1, 1))


def left(x):
    n = x.shape[1]
    return jnp.where(iota(x.shape, 1) == 0, 0.0, pltpu.roll(x, 1, 1))


def weigh(weights, terms):
    total = None
    for w, t in zip(weights, terms):
        if t is not None:
            total = w * t if total is None else total + w * t
    return total


def refine_rows(x, keep):
    m2, m1, p1, p2 = (row(x, s)[:keep] for s in (-2, -1, 1, 2))
    x = x[:keep]
    return weigh(EVEN, (m2, m1, x, p1)), weigh(ODD, (m1, x, p1, p2))


def turn_blocks(x):
    lane = iota((8, 128), 1)
    low = lane < 64
    even = (lane // 32) % 2 == 0
    y0 = jnp.where(low, x[0], pltpu.roll(x[2], 64, 1))
    y2 = jnp.where(low, pltpu.roll(x[0], 64, 1), x[2])
    y1 = jnp.where(low, x[1], pltpu.roll(x[3], 64, 1))
    y3 = jnp.where(low, pltpu.roll(x[1], 64, 1), x[3])
    out = []
    for a, b in ((y0, y1), (y2, y3)):
        out.append(jnp.where(even, a, pltpu.roll(b, 32, 1)))
        out.append(jnp.where(even, pltpu.roll(a, 96, 1), b))
    return out


def restrict(total, matrix):
    high, low = split(total)
    parts = []
    for b in range(4):
        window = slice(256 * b, 256 * b + 256)
        parts.append(dot(high[:, window], matrix) + dot(low[:, window], matrix))
    return jnp.concatenate(parts, axis=1)


def fine_columns(high, low, matrix_ref):
    parts = []
    for b in range(-1, 4):
        window = slice(max(128 * b, 0), min(128 * b + 256, NX))
        if b == -1:
            matrix = matrix_ref[128:256, :]
        elif b == 3:
            matrix = matrix_ref[0:128, :]
        else:
            matrix = matrix_ref[...]
        parts.append((b, window, matrix))
    return [dot(high[:, w], m) + dot(low[:, w], m) for _, w, m in parts]


def refined_rows(x, matrix_ref):
    high, low = split(x)
    parts = []
    parts.append((high[:, :128], low[:, :128], matrix_ref[128:256, 128:256]))
    for b in range(3):
        w = slice(128 * b, 128 * b + 256)
        parts.append((high[:, w], low[:, w], matrix_ref[...]))
    parts.append((high[:, 384:], low[:, 384:], matrix_ref[0:128, 0:128]))
    return jnp.concatenate([dot(h, m) + dot(l, m) for h, l, m in parts], axis=1)


def heat_mean(planes, keep, matrix_ref):
    high, low = split(jnp.concatenate(planes, axis=0))
    sums = []
    for t in fine_columns(high, low, matrix_ref):
        q = t * (1.0 + 0.5 * t)
        q = q[:, :128] + q[:, 128:]
        sums.append(sum(q[keep * j : keep * j + keep] for j in range(len(planes))))
    rolled = [pltpu.roll(s, 64, 1) for s in sums]
    low_half = iota((keep, 128), 1) < 64
    return 0.125 * jnp.concatenate(
        [jnp.where(low_half, rolled[c], rolled[c + 1]) for c in range(4)], axis=1
    )


def upwind(speed, positive, below, above):
    return speed * jnp.where(positive, below, above)


def gathered(c_ref, u_ref, d_ref, f, m):
    first = iota((8, NX), 0) < 4
    d = d_ref[2 * f + m // 2]
    u = u_ref[2 * f + m // 2]
    if m % 2 == 0:
        rim = jnp.where(first, d, pltpu.roll(u, 4, 0))
    else:
        rim = jnp.where(first, pltpu.roll(d, 4, 0), u)
    return jnp.concatenate([c_ref[f, m], rim], axis=0)


def wide(ref, tile, rows):
    return jnp.concatenate([ref[tile, rows, :], ref[tile + 1, rows, :]], axis=-1)


def pack_kernel(flow_ref, heat_ref, salt_ref, restrict_ref, a_ref, g_ref, mean_ref, plane_ref, strip):
    z = lax.axis_index("gz")
    for lv in range(2):
        block = jnp.concatenate([flow_ref[0, lv], flow_ref[1, lv], flow_ref[2, lv], heat_ref[lv]], axis=0)
        turned = block.T
        for j in range(16):
            piece = turned[8 * j : 8 * j + 8]
            a_ref[j, 0, lv] = piece
            a_ref[j, 1, lv] = piece
    for l in range(4):
        for c in range(8):
            strip[c, l] = salt_ref[l, :, 128 * c : 128 * c + 128]
    for l in range(4):
        for q in range(2):
            for c in range(8):
                plane_ref[l, q, :, 128 * c : 128 * c + 128] = strip[c, l, pl.ds(q, 8, stride=2), :]
    totals = []
    for m in range(2):
        totals.append(sum(plane_ref[2 * m + p, q] for p in range(2) for q in range(2)))
    means = restrict(jnp.concatenate(totals, axis=0), restrict_ref[...])
    for m in range(2):
        mean_ref[m] = means[8 * m : 8 * m + 8]
        g_ref[8 + m] = means[8 * m : 8 * m + 8]
    for near in range(2):
        level = jnp.where(z == 0, 3 - near, near)
        for q in range(2):
            plane = plane_ref[level, q]
            for h in range(2):
                g_ref[4 * near + 2 * q + h] = plane[:, 512 * h : 512 * h + 512]


def turn_kernel(d_ref, salt_ref, mean_ref, g_ref, c_ref, up_ref, down_ref):
    z = lax.axis_index("gz")
    for m in range(4):
        for b in range(4):
            tiles = turn_blocks([d_ref[4 * b + j, m] for j in range(4)])
            for f in range(4):
                c_ref[f, m, :, 128 * b : 128 * b + 128] = tiles[f]
        own = mean_ref[m % 2]
        other = g_ref[8 + m % 2]
        c_ref[4, m] = jnp.where(z == m // 2, own, other)
    first = iota((8, NX), 0) < 4
    for f in range(5):
        for p in range(2):
            a = c_ref[f, 2 * p]
            b = c_ref[f, 2 * p + 1]
            down_ref[2 * f + p] = jnp.where(first, a, pltpu.roll(b, 4, 0))
            up_ref[2 * f + p] = jnp.where(first, pltpu.roll(a, 4, 0), b)
    down_ref[12] = jnp.zeros((8, NX), F32)
    up_ref[12] = jnp.zeros((8, NX), F32)
    for h in range(2):
        w = slice(512 * h, 512 * h + 512)
        for l in range(4):
            down_ref[10 + h, 2 * l : 2 * l + 2, :] = salt_ref[l, 0:2, w]
            up_ref[10 + h, 2 * l : 2 * l + 2, :] = salt_ref[l, 14:16, w]
        down_ref[12, h : h + 1, :] = g_ref[h, 0:1, :]
        up_ref[12, h : h + 1, :] = g_ref[2 + h, 7:8, :]


def coarse_rate(q, below, above, speeds, positives, diffusion, keep):
    x = q[:keep]
    up = (above - x, right(x) - x, row(q, 1)[:keep] - x)
    down = (x - below, x - left(x), x - row(q, -1)[:keep])
    spread = (up[0] - down[0]) + (up[1] - down[1]) + (up[2] - down[2])
    carried = sum(upwind(a, s, d, u) for a, s, d, u in zip(speeds, positives, down, up))
    return diffusion * spread - carried


def salt_step(x, below, above, before, after, speeds):
    up = (above - x, after - x, right(x) - x)
    down = (x - below, x - before, x - left(x))
    spread = (up[0] - down[0]) + (up[1] - down[1]) + (up[2] - down[2])
    carried = sum(upwind(a, a > 0, d, u) for a, d, u in zip(speeds, down, up))
    return (DT * 0.05 / 0.25) * spread - (DT / 0.5) * carried


def coarse_kernel(
    c_ref, ur_ref, dr_ref, salt_ref, g_ref, refine_ref, refine_split_ref, restrict_ref,
    msg_ref, mid_out_ref, cp, mp, vel,
):
    z = lax.axis_index("gz")
    place = lax.axis_index("gx") * 16 + lax.axis_index("gy")
    zero = jnp.zeros((16, NX), F32)
    for f in range(4):
        for k in (0, 1, 6, 7):
            cp[f, k] = zero
            mp[f, k] = zero
        for m in range(4):
            cp[f, m + 2] = gathered(c_ref, ur_ref, dr_ref, f, m)
    for f in range(3):
        for m in range(2):
            for p in range(2):
                level = weigh(EVEN if p == 0 else ODD, [cp[f, 2 * z + m + p + k] for k in range(4)])
                even, odd = refine_rows(level, 8)
                vel[f, 2 * m + p] = refined_rows(jnp.concatenate([even, odd], axis=0), refine_ref)
    rows16 = iota((16, NX), 0)
    inside = ((rows16 < 8) | (rows16 >= 12) | (place != 127)) & ((rows16 < 12) | (place != 0))
    for m in range(4):
        planes = []
        for p in range(2):
            terms = [cp[3, m + p + k] if 2 <= m + p + k < 6 else None for k in range(4)]
            planes.extend(refine_rows(weigh(EVEN if p == 0 else ODD, terms), 16))
        buoyancy = heat_mean(planes, 16, refine_split_ref) - 0.8 * gathered(c_ref, ur_ref, dr_ref, 4, m)
        speeds = [cp[f, m + 2] for f in range(3)]
        positives = [s > 0 for s in speeds]
        for f in range(4):
            q = cp[f, m + 2]
            rate = coarse_rate(q, cp[f, m + 1], cp[f, m + 3], speeds, positives, KINDS[f], 16)
            if f == 0:
                rate = rate + buoyancy
            mid = jnp.where(inside, q + DT * rate, 0.0)
            mp[f, m + 2] = mid
            if f < 3:
                mid_out_ref[f, m] = mid
    line = iota((8, NF), 0)
    totals = []
    for m in range(2):
        total = None
        for p in range(2):
            l = 2 * m + p
            own = [salt_ref[l, q] for q in range(2)]
            following = jnp.where(line == 7, wide(dr_ref, 10, slice(2 * l, 2 * l + 1)), pltpu.roll(own[0], 7, 0))
            preceding = jnp.where(line == 0, wide(ur_ref, 10, slice(2 * l + 1, 2 * l + 2)), pltpu.roll(own[1], 1, 0))
            around = ((preceding, own[1]), (own[0], following))
            for q in range(2):
                near = wide(g_ref, 2 * q, slice(0, 8))
                if l == 0:
                    below = jnp.where(z == 1, near, 0.0)
                else:
                    below = salt_ref[l - 1, q]
                if l == 3:
                    above = jnp.where(z == 0, near, 0.0)
                else:
                    above = salt_ref[l + 1, q]
                speeds = [vel[f, l, 8 * q : 8 * q + 8, :] for f in (0, 2, 1)]
                x = own[q]
                mid = x + salt_step(x, below, above, around[q][0], around[q][1], speeds)
                total = mid if total is None else total + mid
        totals.append(total)
    means = restrict(jnp.concatenate(totals, axis=0), restrict_ref[...])
    for m in range(2):
        planes = []
        for p in range(2):
            level = weigh(EVEN if p == 0 else ODD, [mp[3, 2 * z + m + p + k] for k in range(4)])
            planes.extend(refine_rows(level, 8))
        buoyancy = heat_mean(planes, 8, refine_split_ref) - 0.8 * means[8 * m : 8 * m + 8]
        at = 2 * z + m + 2
        speeds = [mp[f, at, 0:8, :] for f in range(3)]
        positives = [s > 0 for s in speeds]
        ends = []
        for f in range(4):
            q = mp[f, at]
            rate = coarse_rate(q, mp[f, at - 1, 0:8, :], mp[f, at + 1, 0:8, :], speeds, positives, KINDS[f], 8)
            if f == 0:
                rate = rate + buoyancy
            ends.append(0.5 * cp[f, at, 0:8, :] + 0.5 * (q[:8] + DT * rate))
        for b in range(4):
            tiles = turn_blocks([ends[f][:, 128 * b : 128 * b + 128] for f in range(4)])
            for j in range(4):
                msg_ref[4 * b + j, m] = tiles[j]


def salt_kernel(
    c_ref, ur_ref, dr_ref, salt_ref, g_ref, mid_ref, refine_ref, out_ref, cp, ss, sm, vel, near_vel, mv, strip,
):
    z = lax.axis_index("gz")
    place = lax.axis_index("gx") * 16 + lax.axis_index("gy")
    zero = jnp.zeros((16, NX), F32)
    for f in range(3):
        for k in (0, 1, 6, 7):
            cp[f, k] = zero
            mv[f, k] = zero
        for m in range(4):
            cp[f, m + 2] = gathered(c_ref, ur_ref, dr_ref, f, m)
            mv[f, m + 2] = mid_ref[f, m]
    for f in range(3):
        for m in range(2):
            for p in range(2):
                level = weigh(EVEN if p == 0 else ODD, [cp[f, 2 * z + m + p + k] for k in range(4)])
                even, odd = refine_rows(level, 16)
                vel[f, 2 * m + p] = refined_rows(jnp.concatenate([even, odd], axis=0), refine_ref)
        weights = [jnp.where(z == 0, EVEN[k], ODD[k]) for k in range(4)]
        even, odd = refine_rows(weigh(weights, [cp[f, 2 + k] for k in range(4)]), 8)
        near_vel[f] = refined_rows(jnp.concatenate([even, odd], axis=0), refine_ref)
    line = iota((8, NF), 0)
    for q in range(2):
        for l in range(4):
            ss[q, l + 1, 0:8, :] = salt_ref[l, q]
            d = wide(dr_ref, 10, slice(2 * l + q, 2 * l + q + 1))
            u = wide(ur_ref, 10, slice(2 * l + q, 2 * l + q + 1))
            ss[q, l + 1, 8:16, :] = jnp.where(line == 0, d, jnp.where(line == 7, u, 0.0))
        near = wide(g_ref, 2 * q, slice(0, 8))
        if q == 0:
            edge = jnp.concatenate([dr_ref[12, 0:1, :], dr_ref[12, 1:2, :]], axis=-1)
            rim = jnp.where(line == 0, edge, 0.0)
        else:
            edge = jnp.concatenate([ur_ref[12, 0:1, :], ur_ref[12, 1:2, :]], axis=-1)
            rim = jnp.where(line == 7, edge, 0.0)
        whole = jnp.concatenate([near, rim], axis=0)
        ss[q, 0] = jnp.where(z == 1, whole, 0.0)
        ss[q, 5] = jnp.where(z == 0, whole, 0.0)
    line16 = iota((16, NF), 0)
    inside = ((line16 < 8) | (line16 >= 12) | (place != 127)) & ((line16 < 12) | (place != 0))
    for l in range(1, 5):
        pair = [ss[0, l], ss[1, l]]
        around = ((row(pair[1], -1), pair[1]), (pair[0], row(pair[0], 1)))
        for q in range(2):
            speeds = [vel[f, l - 1, 16 * q : 16 * q + 16, :] for f in (0, 2, 1)]
            x = pair[q]
            mid = x + salt_step(x, ss[q, l - 1], ss[q, l + 1], around[q][0], around[q][1], speeds)
            sm[q, l] = jnp.where(inside, mid, 0.0)
    pair = [jnp.where(z == 0, ss[q, 5], ss[q, 0]) for q in range(2)]
    around = ((row(pair[1], -1)[:8], pair[1][:8]), (pair[0][:8], row(pair[0], 1)[:8]))
    for q in range(2):
        far = wide(g_ref, 4 + 2 * q, slice(0, 8))
        below = jnp.where(z == 0, ss[q, 4, 0:8, :], far)
        above = jnp.where(z == 0, far, ss[q, 1, 0:8, :])
        speeds = [near_vel[f, 8 * q : 8 * q + 8, :] for f in (0, 2, 1)]
        x = pair[q][:8]
        mid = x + salt_step(x, below, above, around[q][0], around[q][1], speeds)
        sm[q, 0, 0:8, :] = jnp.where(z == 1, mid, 0.0)
        sm[q, 5, 0:8, :] = jnp.where(z == 0, mid, 0.0)
    for f in range(3):
        for m in range(2):
            for p in range(2):
                level = weigh(EVEN if p == 0 else ODD, [mv[f, 2 * z + m + p + k] for k in range(4)])
                even, odd = refine_rows(level, 8)
                vel[f, 2 * m + p, 0:16, :] = refined_rows(jnp.concatenate([even, odd], axis=0), refine_ref)
    for l in range(1, 5):
        pair = [sm[0, l], sm[1, l]]
        around = ((row(pair[1], -1)[:8], pair[1][:8]), (pair[0][:8], row(pair[0], 1)[:8]))
        for q in range(2):
            speeds = [vel[f, l - 1, 8 * q : 8 * q + 8, :] for f in (0, 2, 1)]
            x = pair[q][:8]
            step = salt_step(x, sm[q, l - 1, 0:8, :], sm[q, l + 1, 0:8, :], around[q][0], around[q][1], speeds)
            end = 0.5 * ss[q, l, 0:8, :] + 0.5 * (x + step)
            for c in range(8):
                strip[c, l - 1, pl.ds(q, 8, stride=2), :] = end[:, 128 * c : 128 * c + 128]
        for c in range(8):
            out_ref[l - 1, :, 128 * c : 128 * c + 128] = strip[c, l - 1]


def unpack_kernel(x_ref, flow_ref, heat_ref):
    for lv in range(2):
        turned = jnp.concatenate([x_ref[j, lv] for j in range(16)], axis=0).T
        for f in range(3):
            flow_ref[f, lv] = turned[32 * f : 32 * f + 32]
        heat_ref[lv] = turned[96:128]


def call(kernel, name, outs, scratch=(), limit=None):
    return pl.pallas_call(
        kernel,
        name=name,
        out_shape=[jax.ShapeDtypeStruct(s, F32) for s in outs],
        scratch_shapes=list(scratch),
    )


def on_device(flow, heat, salt):
    ring = 128
    up = [(i, i + 1) for i in range(ring - 1)]
    down = [(j, i) for i, j in up]
    refine = jnp.asarray(REFINE, BF16)
    refine_split = jnp.asarray(REFINE_SPLIT, BF16)
    restrict_m = jnp.asarray(RESTRICT, BF16)
    vmem = pltpu.VMEM
    a, g, means, planes = call(
        pack_kernel,
        "pack",
        [(16, 2, 2, 8, 128), (10, 8, NX), (2, 8, NX), (4, 2, 8, NF)],
        [vmem((8, 4, 16, 128), F32)],
    )(flow, heat, salt, restrict_m)
    g = lax.ppermute(g, "gz", [(0, 1), (1, 0)])
    d = lax.all_to_all(a.reshape(32, 2, 8, 128), ("gy", "gz"), 0, 0, tiled=True)
    c, u, w = call(turn_kernel, "turn", [(5, 4, 8, NX), (13, 8, NX), (13, 8, NX)])(
        d.reshape(16, 4, 8, 128), salt, means, g
    )
    u = lax.ppermute(u, ("gx", "gy"), up)
    w = lax.ppermute(w, ("gx", "gy"), down)
    msg, mid = call(
        coarse_kernel,
        "coarse",
        [(16, 2, 8, 128), (3, 4, 16, NX)],
        [vmem((4, 8, 16, NX), F32), vmem((4, 8, 16, NX), F32), vmem((3, 4, 16, NF), F32)],
    )(c, u, w, planes, g, refine, refine_split, restrict_m)
    back = lax.all_to_all(msg, "gy", 0, 0, tiled=True)
    (salt_end,) = call(
        salt_kernel,
        "salt",
        [(4, 16, NF)],
        [
            vmem((3, 8, 16, NX), F32),
            vmem((2, 6, 16, NF), F32),
            vmem((2, 6, 16, NF), F32),
            vmem((3, 4, 32, NF), F32),
            vmem((3, 16, NF), F32),
            vmem((3, 8, 16, NX), F32),
            vmem((8, 4, 16, 128), F32),
        ],
    )(c, u, w, planes, g, mid, refine)
    flow_end, heat_end = call(unpack_kernel, "unpack", [(3, 2, 32, 128), (2, 32, 128)])(back)
    return flow_end, heat_end, salt_end


def solution(mesh):
    specs = (P(None, "gz", "gy", "gx"), P("gz", "gy", "gx"), P("gz", ("gx", "gy"), None))
    return jax.shard_map(on_device, mesh=mesh, in_specs=specs, out_specs=specs, check_vma=False)
```

```python
import jax
import jax.numpy as jnp
import numpy as np
from jax import lax
from jax.experimental import pallas as pl
from jax.experimental.pallas import tpu as pltpu
from jax.sharding import PartitionSpec as P

F32 = jnp.float32
BF16 = jnp.bfloat16
DT = 0.1
EVEN = (-0.0390625, 0.2734375, 0.8203125, -0.0546875)
ODD = (-0.0546875, 0.8203125, 0.2734375, -0.0390625)
KINDS = (0.2, 0.2, 0.2, 0.15)
NX = 512
NF = 1024


def refine_matrix():
    matrix = np.zeros((256, 256), np.float32)
    for n in range(256):
        i = 64 + n // 2
        for k in range(4):
            matrix[i + k - (2 if n % 2 == 0 else 1), n] = (EVEN if n % 2 == 0 else ODD)[k]
    return matrix


def restrict_matrix():
    matrix = np.zeros((256, 128), np.float32)
    for n in range(256):
        matrix[n, n // 2] = 0.125
    return matrix


REFINE = refine_matrix()
REFINE_SPLIT = np.concatenate([REFINE[:, 0::2], REFINE[:, 1::2]], axis=1)
RESTRICT = restrict_matrix()


def dot(a, b):
    return jnp.dot(a, b, preferred_element_type=F32)


def split(x):
    high = x.astype(BF16)
    return high, (x - high.astype(F32)).astype(BF16)


def row(x, s):
    n = x.shape[0]
    return x if s % n == 0 else pltpu.roll(x, (-s) % n, 0)


def iota(shape, axis):
    return lax.broadcasted_iota(jnp.int32, shape, axis)


def right(x):
    n = x.shape[1]
    return jnp.where(iota(x.shape, 1) == n - 1, 0.0, pltpu.roll(x, n - 1, 1))


def left(x):
    n = x.shape[1]
    return jnp.where(iota(x.shape, 1) == 0, 0.0, pltpu.roll(x, 1, 1))


def weigh(weights, terms):
    total = None
    for w, t in zip(weights, terms):
        if t is not None:
            total = w * t if total is None else total + w * t
    return total


def refine_rows(x, keep):
    m2, m1, p1, p2 = (row(x, s)[:keep] for s in (-2, -1, 1, 2))
    x = x[:keep]
    return weigh(EVEN, (m2, m1, x, p1)), weigh(ODD, (m1, x, p1, p2))


def turn_blocks(x):
    lane = iota((8, 128), 1)
    low = lane < 64
    even = (lane // 32) % 2 == 0
    y0 = jnp.where(low, x[0], pltpu.roll(x[2], 64, 1))
    y2 = jnp.where(low, pltpu.roll(x[0], 64, 1), x[2])
    y1 = jnp.where(low, x[1], pltpu.roll(x[3], 64, 1))
    y3 = jnp.where(low, pltpu.roll(x[1], 64, 1), x[3])
    out = []
    for a, b in ((y0, y1), (y2, y3)):
        out.append(jnp.where(even, a, pltpu.roll(b, 32, 1)))
        out.append(jnp.where(even, pltpu.roll(a, 96, 1), b))
    return out


def restrict(total, matrix):
    high, low = split(total)
    parts = []
    for b in range(4):
        window = slice(256 * b, 256 * b + 256)
        parts.append(dot(high[:, window], matrix) + dot(low[:, window], matrix))
    return jnp.concatenate(parts, axis=1)


def fine_columns(high, low, matrix_ref):
    parts = []
    for b in range(-1, 4):
        window = slice(max(128 * b, 0), min(128 * b + 256, NX))
        if b == -1:
            matrix = matrix_ref[128:256, :]
        elif b == 3:
            matrix = matrix_ref[0:128, :]
        else:
            matrix = matrix_ref[...]
        parts.append((b, window, matrix))
    return [dot(high[:, w], m) + dot(low[:, w], m) for _, w, m in parts]


def refined_rows(x, matrix_ref):
    high, low = split(x)
    parts = []
    parts.append((high[:, :128], low[:, :128], matrix_ref[128:256, 128:256]))
    for b in range(3):
        w = slice(128 * b, 128 * b + 256)
        parts.append((high[:, w], low[:, w], matrix_ref[...]))
    parts.append((high[:, 384:], low[:, 384:], matrix_ref[0:128, 0:128]))
    return jnp.concatenate([dot(h, m) + dot(l, m) for h, l, m in parts], axis=1)


def heat_mean(planes, keep, matrix_ref):
    high, low = split(jnp.concatenate(planes, axis=0))
    sums = []
    for t in fine_columns(high, low, matrix_ref):
        q = t * (1.0 + 0.5 * t)
        q = q[:, :128] + q[:, 128:]
        sums.append(sum(q[keep * j : keep * j + keep] for j in range(len(planes))))
    rolled = [pltpu.roll(s, 64, 1) for s in sums]
    low_half = iota((keep, 128), 1) < 64
    return 0.125 * jnp.concatenate(
        [jnp.where(low_half, rolled[c], rolled[c + 1]) for c in range(4)], axis=1
    )


def upwind(speed, positive, below, above):
    return speed * jnp.where(positive, below, above)


def wide(ref, tile, rows):
    return jnp.concatenate([ref[tile, rows, :], ref[tile + 1, rows, :]], axis=-1)


def pack_kernel(flow_hbm, heat_hbm, salt_hbm, restrict_hbm, a_ref, g_ref, mean_ref, plane_ref,
                tile, strip, restrict_ref, sems):
    z = lax.axis_index("gz")
    flow_in = [pltpu.make_async_copy(flow_hbm, tile.at[pl.ds(0, 3)], sems.at[0])]
    flow_in.append(pltpu.make_async_copy(heat_hbm, tile.at[3], sems.at[1]))
    salt_in = [
        pltpu.make_async_copy(salt_hbm.at[:, :, pl.ds(128 * c, 128)], strip.at[c], sems.at[3 + c]) for c in range(8)
    ]
    salt_in.append(pltpu.make_async_copy(restrict_hbm, restrict_ref, sems.at[2]))
    for copy in flow_in + salt_in:
        copy.start()
    for copy in flow_in:
        copy.wait()
    for lv in range(2):
        turned = jnp.concatenate([tile[f, lv] for f in range(4)], axis=0).T
        for j in range(16):
            piece = turned[8 * j : 8 * j + 8]
            a_ref[j, 0, lv] = piece
            a_ref[j, 1, lv] = piece
    for copy in salt_in:
        copy.wait()
    for l in range(4):
        for q in range(2):
            for c in range(8):
                plane_ref[l, q, :, 128 * c : 128 * c + 128] = strip[c, l, pl.ds(q, 8, stride=2), :]
    totals = []
    for m in range(2):
        totals.append(sum(plane_ref[2 * m + p, q] for p in range(2) for q in range(2)))
    means = restrict(jnp.concatenate(totals, axis=0), restrict_ref[...])
    for m in range(2):
        mean_ref[m] = means[8 * m : 8 * m + 8]
        g_ref[8 + m] = means[8 * m : 8 * m + 8]
    for near in range(2):
        level = jnp.where(z == 0, 3 - near, near)
        for q in range(2):
            plane = plane_ref[level, q]
            for h in range(2):
                g_ref[4 * near + 2 * q + h] = plane[:, 512 * h : 512 * h + 512]


def mean_of(mean_ref, g_ref, z, m):
    return jnp.where(z == m // 2, mean_ref[m % 2], g_ref[8 + m % 2])


def send_kernel(d_ref, plane_ref, mean_ref, g_ref, c_ref, near_ref, far_ref, up_ref, down_ref):
    z = lax.axis_index("gz")
    leads = lax.rem(lax.axis_index("gy"), 2) == 0
    for m in range(4):
        for b in range(4):
            tiles = turn_blocks([d_ref[4 * b + j, m] for j in range(4)])
            for f in range(4):
                c_ref[f, m, :, 128 * b : 128 * b + 128] = tiles[f]
        c_ref[4, m] = mean_of(mean_ref, g_ref, z, m)
    first = iota((8, NX), 0) < 4
    for f in range(5):
        for p in range(2):
            a = c_ref[f, 2 * p]
            b = c_ref[f, 2 * p + 1]
            down_ref[2 * f + p] = jnp.where(first, a, pltpu.roll(b, 4, 0))
            up_ref[2 * f + p] = jnp.where(first, pltpu.roll(a, 4, 0), b)
    down_ref[12] = jnp.zeros((8, NX), F32)
    up_ref[12] = jnp.zeros((8, NX), F32)
    for h in range(2):
        w = slice(512 * h, 512 * h + 512)
        for l in range(4):
            for q in range(2):
                k = 2 * l + q
                down_ref[10 + h, k : k + 1, :] = plane_ref[l, q, 0:1, w]
                up_ref[10 + h, k : k + 1, :] = plane_ref[l, q, 7:8, w]
        down_ref[12, h : h + 1, :] = g_ref[h, 0:1, :]
        up_ref[12, h : h + 1, :] = g_ref[2 + h, 7:8, :]
    for t in range(13):
        up = up_ref[t]
        down = down_ref[t]
        near_ref[t] = jnp.where(leads, up, down)
        far_ref[t] = jnp.where(leads, down, up)


def coarse_rate(q, below, above, speeds, positives, diffusion, keep):
    x = q[:keep]
    up = (above - x, right(x) - x, row(q, 1)[:keep] - x)
    down = (x - below, x - left(x), x - row(q, -1)[:keep])
    spread = (up[0] - down[0]) + (up[1] - down[1]) + (up[2] - down[2])
    carried = sum(upwind(a, s, d, u) for a, s, d, u in zip(speeds, positives, down, up))
    return diffusion * spread - carried


def salt_step(x, below, above, before, after, speeds):
    up = (above - x, after - x, right(x) - x)
    down = (x - below, x - before, x - left(x))
    spread = (up[0] - down[0]) + (up[1] - down[1]) + (up[2] - down[2])
    carried = sum(upwind(a, a > 0, d, u) for a, d, u in zip(speeds, down, up))
    return (DT * 0.05 / 0.25) * spread - (DT / 0.5) * carried


def edge_row(ref, k):
    whole = jnp.concatenate([ref[10, k : k + 1, :], ref[11, k : k + 1, :]], axis=-1)
    return jnp.broadcast_to(whole, (8, NF))


def near_edge(ref):
    whole = jnp.concatenate([ref[12, 0:1, :], ref[12, 1:2, :]], axis=-1)
    return jnp.broadcast_to(whole, (8, NF))


def levels_of(fields, f, start, parity):
    return weigh(EVEN if parity == 0 else ODD, [fields[f, start + parity + k] for k in range(4)])


def rim_of(ur_ref, dr_ref, f, m):
    first = iota((8, NX), 0) < 4
    d = dr_ref[2 * f + m // 2]
    u = ur_ref[2 * f + m // 2]
    if m % 2 == 0:
        return jnp.where(first, d, pltpu.roll(u, 4, 0))
    return jnp.where(first, pltpu.roll(d, 4, 0), u)


def coarse_kernel(
    c_ref, near_ref, far_ref, plane_ref, g_ref, refine_ref, refine_split_ref, restrict_ref,
    msg_ref, cp, mp, salt_mid, ur_ref, dr_ref, vel,
):
    z = lax.axis_index("gz")
    leads = lax.rem(lax.axis_index("gy"), 2) == 0
    place = lax.axis_index("gx") * 16 + lax.axis_index("gy")
    for t in range(13):
        near = near_ref[t]
        far = far_ref[t]
        ur_ref[t] = jnp.where(leads, far, near)
        dr_ref[t] = jnp.where(leads, near, far)
    zero = jnp.zeros((16, NX), F32)
    for f in range(4):
        for k in (0, 1, 6, 7):
            cp[f, k] = zero
            mp[f, k] = zero
        for m in range(4):
            cp[f, m + 2, 0:8, :] = c_ref[f, m]
            cp[f, m + 2, 8:16, :] = rim_of(ur_ref, dr_ref, f, m)
    for f in range(3):
        for m in range(2):
            for p in range(2):
                even, odd = refine_rows(levels_of(cp, f, 2 * z + m, p), 8)
                vel[f, 2 * m + p] = refined_rows(jnp.concatenate([even, odd], axis=0), refine_ref)
    rows16 = iota((16, NX), 0)
    inside = ((rows16 < 8) | (rows16 >= 12) | (place != 127)) & ((rows16 < 12) | (place != 0))
    for m in range(4):
        planes = []
        for p in range(2):
            terms = [cp[3, m + p + k] if 2 <= m + p + k < 6 else None for k in range(4)]
            planes.extend(refine_rows(weigh(EVEN if p == 0 else ODD, terms), 16))
        salt_mean = jnp.concatenate([c_ref[4, m], rim_of(ur_ref, dr_ref, 4, m)], axis=0)
        buoyancy = heat_mean(planes, 16, refine_split_ref) - 0.8 * salt_mean
        speeds = [cp[f, m + 2] for f in range(3)]
        positives = [s > 0 for s in speeds]
        for f in range(4):
            q = cp[f, m + 2]
            rate = coarse_rate(q, cp[f, m + 1], cp[f, m + 3], speeds, positives, KINDS[f], 16)
            if f == 0:
                rate = rate + buoyancy
            mp[f, m + 2] = jnp.where(inside, q + DT * rate, 0.0)
    line = iota((8, NF), 0)
    totals = []
    for m in range(2):
        total = None
        for p in range(2):
            l = 2 * m + p
            own = [plane_ref[l, q] for q in range(2)]
            following = jnp.where(line == 7, edge_row(dr_ref, 2 * l), pltpu.roll(own[0], 7, 0))
            preceding = jnp.where(line == 0, edge_row(ur_ref, 2 * l + 1), pltpu.roll(own[1], 1, 0))
            around = ((preceding, own[1]), (own[0], following))
            for q in range(2):
                near = wide(g_ref, 2 * q, slice(0, 8))
                below = jnp.where(z == 1, near, 0.0) if l == 0 else plane_ref[l - 1, q]
                above = jnp.where(z == 0, near, 0.0) if l == 3 else plane_ref[l + 1, q]
                speeds = [vel[f, l, 8 * q : 8 * q + 8, :] for f in (0, 2, 1)]
                x = own[q]
                mid = x + salt_step(x, below, above, around[q][0], around[q][1], speeds)
                salt_mid[l, q] = mid
                total = mid if total is None else total + mid
        totals.append(total)
    means = restrict(jnp.concatenate(totals, axis=0), restrict_ref[...])
    for m in range(2):
        planes = []
        for p in range(2):
            planes.extend(refine_rows(levels_of(mp, 3, 2 * z + m, p), 8))
        buoyancy = heat_mean(planes, 8, refine_split_ref) - 0.8 * means[8 * m : 8 * m + 8]
        at = 2 * z + m + 2
        speeds = [mp[f, at, 0:8, :] for f in range(3)]
        positives = [s > 0 for s in speeds]
        ends = []
        for f in range(4):
            q = mp[f, at]
            rate = coarse_rate(q, mp[f, at - 1, 0:8, :], mp[f, at + 1, 0:8, :], speeds, positives, KINDS[f], 8)
            if f == 0:
                rate = rate + buoyancy
            ends.append(0.5 * cp[f, at, 0:8, :] + 0.5 * (q[:8] + DT * rate))
        for b in range(4):
            tiles = turn_blocks([ends[f][:, 128 * b : 128 * b + 128] for f in range(4)])
            for j in range(4):
                msg_ref[4 * b + j, m] = tiles[j]


def salt_kernel(
    cp, mv, salt_mid_ref, plane_ref, ur_ref, dr_ref, g_ref, refine_ref, out_ref, vel, near_vel, strip,
):
    z = lax.axis_index("gz")
    place = lax.axis_index("gx") * 16 + lax.axis_index("gy")
    top = iota((8, NX), 0) == 0
    for f in range(3):
        rims = []
        for m in range(2):
            for p in range(2):
                even, odd = refine_rows(levels_of(cp, f, 2 * z + m, p), 16)
                rims.append(jnp.where(top, even[8:], odd[8:]))
        weights = [jnp.where(z == 0, EVEN[k], ODD[k]) for k in range(4)]
        rims.extend(refine_rows(weigh(weights, [cp[f, 2 + k] for k in range(4)]), 8))
        near_vel[f] = refined_rows(jnp.concatenate(rims, axis=0), refine_ref)
    for f in range(3):
        for m in range(2):
            for p in range(2):
                even, odd = refine_rows(levels_of(mv, f, 2 * z + m, p), 8)
                vel[f, 2 * m + p] = refined_rows(jnp.concatenate([even, odd], axis=0), refine_ref)
    line = iota((8, NF), 0)
    rim = [jnp.where(line == 0, edge_row(dr_ref, 2 * l), edge_row(ur_ref, 2 * l + 1)) for l in range(4)]
    near_rim = jnp.where(line == 0, near_edge(dr_ref), near_edge(ur_ref))
    bottom = jnp.where(z == 1, near_rim, 0.0)
    roof = jnp.where(z == 0, near_rim, 0.0)
    alive = ((line != 0) | (place != 127)) & ((line != 7) | (place != 0))
    rim_mid = []
    for l in range(4):
        before = jnp.where(line == 0, pltpu.roll(plane_ref[l, 1], 1, 0), edge_row(ur_ref, 2 * l))
        after = jnp.where(line == 0, edge_row(dr_ref, 2 * l + 1), pltpu.roll(plane_ref[l, 0], 7, 0))
        speeds = [near_vel[f, 8 * l : 8 * l + 8, :] for f in (0, 2, 1)]
        below = bottom if l == 0 else rim[l - 1]
        above = roof if l == 3 else rim[l + 1]
        mid = rim[l] + salt_step(rim[l], below, above, before, after, speeds)
        rim_mid.append(jnp.where(alive, mid, 0.0))
    near = [wide(g_ref, 2 * q, slice(0, 8)) for q in range(2)]
    before = jnp.where(line == 0, near_edge(ur_ref), pltpu.roll(near[1], 1, 0))
    after = jnp.where(line == 7, near_edge(dr_ref), pltpu.roll(near[0], 7, 0))
    around = ((before, near[1]), (near[0], after))
    near_mid = []
    for q in range(2):
        far = wide(g_ref, 4 + 2 * q, slice(0, 8))
        below = jnp.where(z == 0, plane_ref[3, q], far)
        above = jnp.where(z == 0, far, plane_ref[0, q])
        speeds = [near_vel[f, 32 + 8 * q : 40 + 8 * q, :] for f in (0, 2, 1)]
        near_mid.append(near[q] + salt_step(near[q], below, above, around[q][0], around[q][1], speeds))
    for l in range(4):
        pair = [salt_mid_ref[l, q] for q in range(2)]
        before = pltpu.roll(jnp.where(line == 7, rim_mid[l], pair[1]), 1, 0)
        after = pltpu.roll(jnp.where(line == 0, rim_mid[l], pair[0]), 7, 0)
        around = ((before, pair[1]), (pair[0], after))
        for q in range(2):
            speeds = [vel[f, l, 8 * q : 8 * q + 8, :] for f in (0, 2, 1)]
            below = jnp.where(z == 1, near_mid[q], 0.0) if l == 0 else salt_mid_ref[l - 1, q]
            above = jnp.where(z == 0, near_mid[q], 0.0) if l == 3 else salt_mid_ref[l + 1, q]
            x = pair[q]
            step = salt_step(x, below, above, around[q][0], around[q][1], speeds)
            end = 0.5 * plane_ref[l, q] + 0.5 * (x + step)
            for c in range(8):
                strip[c, l, pl.ds(q, 8, stride=2), :] = end[:, 128 * c : 128 * c + 128]
        for c in range(8):
            out_ref[l, :, 128 * c : 128 * c + 128] = strip[c, l]


def unpack_kernel(x_ref, flow_ref, heat_ref):
    for lv in range(2):
        turned = jnp.concatenate([x_ref[j, lv] for j in range(16)], axis=0).T
        for f in range(3):
            flow_ref[f, lv] = turned[32 * f : 32 * f + 32]
        heat_ref[lv] = turned[96:128]


SPACES = {"h": pl.BlockSpec(memory_space=pltpu.HBM), "v": pl.BlockSpec(memory_space=pltpu.VMEM)}


def call(kernel, name, ins, outs, scratch=()):
    return pl.pallas_call(
        kernel,
        name=name,
        in_specs=[SPACES[letter] for letter in ins],
        out_specs=[SPACES["v"] for _ in outs],
        out_shape=[jax.ShapeDtypeStruct(s, F32) for s in outs],
        scratch_shapes=list(scratch),
        compiler_params=pltpu.CompilerParams(vmem_limit_bytes=16 * 2**20),
    )


def swap(x, axes, n, start):
    pairs = []
    for i in range(start, n - 1, 2):
        pairs += [(i, i + 1), (i + 1, i)]
    return lax.ppermute(x, axes, pairs)


def on_device(flow, heat, salt):
    vmem = pltpu.VMEM
    refine = jnp.asarray(REFINE, BF16)
    refine_split = jnp.asarray(REFINE_SPLIT, BF16)
    restrict_m = jnp.asarray(RESTRICT, BF16)
    a, g, means, planes = call(
        pack_kernel,
        "pack",
        "hhhh",
        [(16, 2, 2, 8, 128), (10, 8, NX), (2, 8, NX), (4, 2, 8, NF)],
        [
            vmem((4, 2, 32, 128), F32),
            vmem((8, 4, 16, 128), F32),
            vmem((256, 128), BF16),
            pltpu.SemaphoreType.DMA((11,)),
        ],
    )(flow, heat, salt, restrict_m)
    g = swap(g, "gz", 2, 0)
    d = lax.all_to_all(a.reshape(32, 2, 8, 128), ("gy", "gz"), 0, 0, tiled=True)
    rims = [(13, 8, NX)] * 2
    c, near, far, _, _ = call(send_kernel, "send", "vvvv", [(5, 4, 8, NX)] + rims + rims)(
        d.reshape(16, 4, 8, 128), planes, means, g
    )
    near = swap(near, ("gx", "gy"), 128, 0)
    far = swap(far, ("gx", "gy"), 128, 1)
    fields = [(4, 8, 16, NX)] * 2
    msg, cp, mp, salt_mid, u, v = call(
        coarse_kernel,
        "coarse",
        "vvvvvvvv",
        [(16, 2, 8, 128)] + fields + [(4, 2, 8, NF)] + rims,
        [vmem((3, 4, 16, NF), F32)],
    )(c, near, far, planes, g, refine, refine_split, restrict_m)
    back = lax.all_to_all(msg, "gy", 0, 0, tiled=True)
    (salt_end,) = call(
        salt_kernel,
        "salt",
        "vvvvvvvv",
        [(4, 16, NF)],
        [vmem((3, 4, 16, NF), F32), vmem((3, 48, NF), F32), vmem((8, 4, 16, 128), F32)],
    )(cp, mp, salt_mid, planes, u, v, g, refine)
    flow_end, heat_end = call(unpack_kernel, "unpack", "v", [(3, 2, 32, 128), (2, 32, 128)])(back)
    return flow_end, heat_end, salt_end


def solution(mesh):
    specs = (P(None, "gz", "gy", "gx"), P("gz", "gy", "gx"), P("gz", ("gx", "gy"), None))
    return jax.shard_map(on_device, mesh=mesh, in_specs=specs, out_specs=specs, check_vma=False)
```

```python
import jax
import jax.numpy as jnp
import numpy as np
from jax import lax
from jax.experimental import pallas as pl
from jax.experimental.pallas import tpu as pltpu
from jax.sharding import PartitionSpec as P

F32 = jnp.float32
BF16 = jnp.bfloat16
DT = 0.1
EVEN = (-0.0390625, 0.2734375, 0.8203125, -0.0546875)
ODD = (-0.0546875, 0.8203125, 0.2734375, -0.0390625)
KINDS = (0.2, 0.2, 0.2, 0.15)
NX = 512
NF = 1024


def refine_matrix():
    matrix = np.zeros((256, 256), np.float32)
    for n in range(256):
        i = 64 + n // 2
        for k in range(4):
            matrix[i + k - (2 if n % 2 == 0 else 1), n] = (EVEN if n % 2 == 0 else ODD)[k]
    return matrix


def restrict_matrix():
    matrix = np.zeros((256, 128), np.float32)
    for n in range(256):
        matrix[n, n // 2] = 0.125
    return matrix


def level_row_matrix(levels, parts):
    rows = np.zeros((2, 16, 16), np.float64)
    for q, weights in enumerate((EVEN, ODD)):
        for i in range(16):
            for k in range(4):
                rows[q, i, (i + k - 2 + q) % 16] = weights[k]
    deep = np.zeros((len(levels), 4), np.float64)
    for n, l in enumerate(levels):
        for k in range(4):
            m = l // 2 + k - 2 + l % 2
            if 0 <= m < 4:
                deep[n, m] = (EVEN, ODD)[l % 2][k]
    whole = np.einsum("lm,qij->lqimj", deep, rows[:, :parts]).reshape(len(levels) * 2 * parts, 64)
    high = whole.astype(np.float32).astype(jnp.bfloat16).astype(np.float64)
    return np.concatenate([high, high, whole - high], axis=1).astype(np.float32)


REFINE = refine_matrix()
REFINE_SPLIT = np.concatenate([REFINE[:, 0::2], REFINE[:, 1::2]], axis=1)
RESTRICT = restrict_matrix()
OWN = np.stack([level_row_matrix(range(4 * z, 4 * z + 4), 8) for z in range(2)])
ALL = level_row_matrix(range(8), 16)


def dot(a, b):
    return jnp.dot(a, b, preferred_element_type=F32)


def split(x):
    high = x.astype(BF16)
    return high, (x - high.astype(F32)).astype(BF16)


def row(x, s):
    n = x.shape[0]
    return x if s % n == 0 else pltpu.roll(x, (-s) % n, 0)


def iota(shape, axis):
    return lax.broadcasted_iota(jnp.int32, shape, axis)


def right(x):
    n = x.shape[1]
    return jnp.where(iota(x.shape, 1) == n - 1, 0.0, pltpu.roll(x, n - 1, 1))


def left(x):
    n = x.shape[1]
    return jnp.where(iota(x.shape, 1) == 0, 0.0, pltpu.roll(x, 1, 1))


def weigh(weights, terms):
    total = None
    for w, t in zip(weights, terms):
        if t is not None:
            total = w * t if total is None else total + w * t
    return total


def refine_rows(x, keep):
    m2, m1, p1, p2 = (row(x, s)[:keep] for s in (-2, -1, 1, 2))
    x = x[:keep]
    return weigh(EVEN, (m2, m1, x, p1)), weigh(ODD, (m1, x, p1, p2))


def turn_blocks(x):
    lane = iota((8, 128), 1)
    low = lane < 64
    even = (lane // 32) % 2 == 0
    y0 = jnp.where(low, x[0], pltpu.roll(x[2], 64, 1))
    y2 = jnp.where(low, pltpu.roll(x[0], 64, 1), x[2])
    y1 = jnp.where(low, x[1], pltpu.roll(x[3], 64, 1))
    y3 = jnp.where(low, pltpu.roll(x[1], 64, 1), x[3])
    out = []
    for a, b in ((y0, y1), (y2, y3)):
        out.append(jnp.where(even, a, pltpu.roll(b, 32, 1)))
        out.append(jnp.where(even, pltpu.roll(a, 96, 1), b))
    return out


def restrict(total, matrix):
    high, low = split(total)
    parts = []
    for b in range(4):
        window = slice(256 * b, 256 * b + 256)
        parts.append(dot(high[:, window], matrix) + dot(low[:, window], matrix))
    return jnp.concatenate(parts, axis=1)


def by_levels_rows(matrix, fields):
    high, low = split(fields.reshape(64, NX))
    return dot(matrix, jnp.concatenate([high, low, high], axis=0))


def windows(x, matrix_ref, halves):
    high, low = split(x)
    parts = []
    for b in range(-1, 4):
        w = slice(max(128 * b, 0), min(128 * b + 256, NX))
        if b == -1:
            matrix = matrix_ref[128:256, :] if halves else matrix_ref[128:256, 128:256]
        elif b == 3:
            matrix = matrix_ref[0:128, :] if halves else matrix_ref[0:128, 0:128]
        else:
            matrix = matrix_ref[...]
        parts.append(dot(jnp.concatenate([high[:, w], low[:, w]], axis=1), jnp.concatenate([matrix, matrix], axis=0)))
    return parts


def refined_rows(x, matrix_ref):
    return jnp.concatenate(windows(x, matrix_ref, False), axis=1)


def heat_mean(x, keep, matrix_ref):
    sums = []
    for t in windows(x, matrix_ref, True):
        total = 0.0
        for j in range(4):
            for h in range(2):
                piece = t[keep * j : keep * j + keep, 128 * h : 128 * h + 128]
                total = total + piece * (1.0 + 0.5 * piece)
        sums.append(pltpu.roll(total, 64, 1))
    low_half = iota((keep, 128), 1) < 64
    return 0.125 * jnp.concatenate([jnp.where(low_half, sums[c], sums[c + 1]) for c in range(4)], axis=1)


def upwind(speed, positive, below, above):
    return speed * jnp.where(positive, below, above)


def wide(ref, tile, rows):
    return jnp.concatenate([ref[tile, rows, :], ref[tile + 1, rows, :]], axis=-1)


def turn_kernel(flow_hbm, heat_hbm, a_ref, tile, sems):
    copies = [pltpu.make_async_copy(flow_hbm, tile.at[pl.ds(0, 3)], sems.at[0])]
    copies.append(pltpu.make_async_copy(heat_hbm, tile.at[3], sems.at[1]))
    for copy in copies:
        copy.start()
    for copy in copies:
        copy.wait()
    for lv in range(2):
        turned = jnp.concatenate([tile[f, lv] for f in range(4)], axis=0).T
        for j in range(16):
            piece = turned[8 * j : 8 * j + 8]
            a_ref[j, 0, lv] = piece
            a_ref[j, 1, lv] = piece


def pack_kernel(salt_ref, restrict_ref, g_ref, mean_ref, plane_ref, strip):
    z = lax.axis_index("gz")
    for l in range(4):
        for c in range(8):
            strip[c, l] = salt_ref[l, :, 128 * c : 128 * c + 128]
    for l in range(4):
        for q in range(2):
            for c in range(8):
                plane_ref[l, q, :, 128 * c : 128 * c + 128] = strip[c, l, pl.ds(q, 8, stride=2), :]
    totals = []
    for m in range(2):
        totals.append(sum(plane_ref[2 * m + p, q] for p in range(2) for q in range(2)))
    means = restrict(jnp.concatenate(totals, axis=0), restrict_ref[...])
    for m in range(2):
        mean_ref[m] = means[8 * m : 8 * m + 8]
        g_ref[8 + m] = means[8 * m : 8 * m + 8]
    for near in range(2):
        level = jnp.where(z == 0, 3 - near, near)
        for q in range(2):
            plane = plane_ref[level, q]
            for h in range(2):
                g_ref[4 * near + 2 * q + h] = plane[:, 512 * h : 512 * h + 512]


def mean_of(mean_ref, g_ref, z, m):
    return jnp.where(z == m // 2, mean_ref[m % 2], g_ref[8 + m % 2])


def send_kernel(d_ref, plane_ref, mean_ref, g_ref, c_ref, near_ref, far_ref, up_ref, down_ref):
    z = lax.axis_index("gz")
    leads = lax.rem(lax.axis_index("gy"), 2) == 0
    for m in range(4):
        for b in range(4):
            tiles = turn_blocks([d_ref[4 * b + j, m] for j in range(4)])
            for f in range(4):
                c_ref[f, m, :, 128 * b : 128 * b + 128] = tiles[f]
        c_ref[4, m] = mean_of(mean_ref, g_ref, z, m)
    first = iota((8, NX), 0) < 4
    for f in range(5):
        for p in range(2):
            a = c_ref[f, 2 * p]
            b = c_ref[f, 2 * p + 1]
            down_ref[2 * f + p] = jnp.where(first, a, pltpu.roll(b, 4, 0))
            up_ref[2 * f + p] = jnp.where(first, pltpu.roll(a, 4, 0), b)
    down_ref[12] = jnp.zeros((8, NX), F32)
    up_ref[12] = jnp.zeros((8, NX), F32)
    for h in range(2):
        w = slice(512 * h, 512 * h + 512)
        for l in range(4):
            for q in range(2):
                k = 2 * l + q
                down_ref[10 + h, k : k + 1, :] = plane_ref[l, q, 0:1, w]
                up_ref[10 + h, k : k + 1, :] = plane_ref[l, q, 7:8, w]
        down_ref[12, h : h + 1, :] = g_ref[h, 0:1, :]
        up_ref[12, h : h + 1, :] = g_ref[2 + h, 7:8, :]
    for t in range(13):
        up = up_ref[t]
        down = down_ref[t]
        near_ref[t] = jnp.where(leads, up, down)
        far_ref[t] = jnp.where(leads, down, up)


def coarse_rate(q, below, above, speeds, positives, diffusion, keep):
    x = q[:keep]
    up = (above - x, right(x) - x, row(q, 1)[:keep] - x)
    down = (x - below, x - left(x), x - row(q, -1)[:keep])
    spread = (up[0] - down[0]) + (up[1] - down[1]) + (up[2] - down[2])
    carried = sum(upwind(a, s, d, u) for a, s, d, u in zip(speeds, positives, down, up))
    return diffusion * spread - carried


def salt_step(x, below, above, before, after, speeds):
    up = (above - x, after - x, right(x) - x)
    down = (x - below, x - before, x - left(x))
    spread = (up[0] - down[0]) + (up[1] - down[1]) + (up[2] - down[2])
    carried = sum(upwind(a, a > 0, d, u) for a, d, u in zip(speeds, down, up))
    return (DT * 0.05 / 0.25) * spread - (DT / 0.5) * carried


def edge_row(ref, k):
    whole = jnp.concatenate([ref[10, k : k + 1, :], ref[11, k : k + 1, :]], axis=-1)
    return jnp.broadcast_to(whole, (8, NF))


def near_edge(ref):
    whole = jnp.concatenate([ref[12, 0:1, :], ref[12, 1:2, :]], axis=-1)
    return jnp.broadcast_to(whole, (8, NF))


def levels_of(fields, f, start, parity):
    return weigh(EVEN if parity == 0 else ODD, [fields[f, start + parity + k] for k in range(4)])


def rim_of(ur_ref, dr_ref, f, m):
    first = iota((8, NX), 0) < 4
    d = dr_ref[2 * f + m // 2]
    u = ur_ref[2 * f + m // 2]
    if m % 2 == 0:
        return jnp.where(first, d, pltpu.roll(u, 4, 0))
    return jnp.where(first, pltpu.roll(d, 4, 0), u)


def coarse_kernel(
    c_ref, near_ref, far_ref, plane_ref, g_ref, refine_ref, refine_split_ref, restrict_ref, own_ref, all_ref,
    msg_ref, cp, mp, salt_mid, ur_ref, dr_ref, vel,
):
    z = lax.axis_index("gz")
    leads = lax.rem(lax.axis_index("gy"), 2) == 0
    place = lax.axis_index("gx") * 16 + lax.axis_index("gy")
    for t in range(13):
        near = near_ref[t]
        far = far_ref[t]
        ur_ref[t] = jnp.where(leads, far, near)
        dr_ref[t] = jnp.where(leads, near, far)
    zero = jnp.zeros((16, NX), F32)
    for f in range(4):
        for k in (0, 1, 6, 7):
            cp[f, k] = zero
            mp[f, k] = zero
        for m in range(4):
            cp[f, m + 2, 0:8, :] = c_ref[f, m]
            cp[f, m + 2, 8:16, :] = rim_of(ur_ref, dr_ref, f, m)
    own_matrix = own_ref[z]
    for f in range(3):
        vel[f] = refined_rows(by_levels_rows(own_matrix, cp[f, 2:6]), refine_ref)
    rows16 = iota((16, NX), 0)
    inside = ((rows16 < 8) | (rows16 >= 12) | (place != 127)) & ((rows16 < 12) | (place != 0))
    heat = by_levels_rows(all_ref[...], cp[3, 2:6])
    for m in range(4):
        salt_mean = jnp.concatenate([c_ref[4, m], rim_of(ur_ref, dr_ref, 4, m)], axis=0)
        buoyancy = heat_mean(heat[64 * m : 64 * m + 64], 16, refine_split_ref) - 0.8 * salt_mean
        speeds = [cp[f, m + 2] for f in range(3)]
        positives = [s > 0 for s in speeds]
        for f in range(4):
            q = cp[f, m + 2]
            rate = coarse_rate(q, cp[f, m + 1], cp[f, m + 3], speeds, positives, KINDS[f], 16)
            if f == 0:
                rate = rate + buoyancy
            mp[f, m + 2] = jnp.where(inside, q + DT * rate, 0.0)
    line = iota((8, NF), 0)
    totals = []
    for m in range(2):
        total = None
        for p in range(2):
            l = 2 * m + p
            own = [plane_ref[l, q] for q in range(2)]
            following = jnp.where(line == 7, edge_row(dr_ref, 2 * l), pltpu.roll(own[0], 7, 0))
            preceding = jnp.where(line == 0, edge_row(ur_ref, 2 * l + 1), pltpu.roll(own[1], 1, 0))
            around = ((preceding, own[1]), (own[0], following))
            for q in range(2):
                near = wide(g_ref, 2 * q, slice(0, 8))
                below = jnp.where(z == 1, near, 0.0) if l == 0 else plane_ref[l - 1, q]
                above = jnp.where(z == 0, near, 0.0) if l == 3 else plane_ref[l + 1, q]
                speeds = [vel[f, 16 * l + 8 * q : 16 * l + 8 * q + 8, :] for f in (0, 2, 1)]
                x = own[q]
                mid = x + salt_step(x, below, above, around[q][0], around[q][1], speeds)
                salt_mid[l, q] = mid
                total = mid if total is None else total + mid
        totals.append(total)
    means = restrict(jnp.concatenate(totals, axis=0), restrict_ref[...])
    heat = by_levels_rows(own_matrix, mp[3, 2:6])
    for m in range(2):
        buoyancy = heat_mean(heat[32 * m : 32 * m + 32], 8, refine_split_ref) - 0.8 * means[8 * m : 8 * m + 8]
        at = 2 * z + m + 2
        speeds = [mp[f, at, 0:8, :] for f in range(3)]
        positives = [s > 0 for s in speeds]
        ends = []
        for f in range(4):
            q = mp[f, at]
            rate = coarse_rate(q, mp[f, at - 1, 0:8, :], mp[f, at + 1, 0:8, :], speeds, positives, KINDS[f], 8)
            if f == 0:
                rate = rate + buoyancy
            ends.append(0.5 * cp[f, at, 0:8, :] + 0.5 * (q[:8] + DT * rate))
        for b in range(4):
            tiles = turn_blocks([ends[f][:, 128 * b : 128 * b + 128] for f in range(4)])
            for j in range(4):
                msg_ref[4 * b + j, m] = tiles[j]


def salt_kernel(
    cp, mv, salt_mid_ref, plane_ref, ur_ref, dr_ref, g_ref, refine_ref, own_ref, out_ref, vel, near_vel, strip,
):
    z = lax.axis_index("gz")
    place = lax.axis_index("gx") * 16 + lax.axis_index("gy")
    top = iota((8, NX), 0) == 0
    for f in range(3):
        rims = []
        for m in range(2):
            for p in range(2):
                even, odd = refine_rows(levels_of(cp, f, 2 * z + m, p), 16)
                rims.append(jnp.where(top, even[8:], odd[8:]))
        weights = [jnp.where(z == 0, EVEN[k], ODD[k]) for k in range(4)]
        rims.extend(refine_rows(weigh(weights, [cp[f, 2 + k] for k in range(4)]), 8))
        near_vel[f] = refined_rows(jnp.concatenate(rims, axis=0), refine_ref)
    for f in range(3):
        vel[f] = refined_rows(by_levels_rows(own_ref[z], mv[f, 2:6]), refine_ref)
    line = iota((8, NF), 0)
    rim = [jnp.where(line == 0, edge_row(dr_ref, 2 * l), edge_row(ur_ref, 2 * l + 1)) for l in range(4)]
    near_rim = jnp.where(line == 0, near_edge(dr_ref), near_edge(ur_ref))
    bottom = jnp.where(z == 1, near_rim, 0.0)
    roof = jnp.where(z == 0, near_rim, 0.0)
    alive = ((line != 0) | (place != 127)) & ((line != 7) | (place != 0))
    rim_mid = []
    for l in range(4):
        before = jnp.where(line == 0, pltpu.roll(plane_ref[l, 1], 1, 0), edge_row(ur_ref, 2 * l))
        after = jnp.where(line == 0, edge_row(dr_ref, 2 * l + 1), pltpu.roll(plane_ref[l, 0], 7, 0))
        speeds = [near_vel[f, 8 * l : 8 * l + 8, :] for f in (0, 2, 1)]
        below = bottom if l == 0 else rim[l - 1]
        above = roof if l == 3 else rim[l + 1]
        mid = rim[l] + salt_step(rim[l], below, above, before, after, speeds)
        rim_mid.append(jnp.where(alive, mid, 0.0))
    near = [wide(g_ref, 2 * q, slice(0, 8)) for q in range(2)]
    before = jnp.where(line == 0, near_edge(ur_ref), pltpu.roll(near[1], 1, 0))
    after = jnp.where(line == 7, near_edge(dr_ref), pltpu.roll(near[0], 7, 0))
    around = ((before, near[1]), (near[0], after))
    near_mid = []
    for q in range(2):
        far = wide(g_ref, 4 + 2 * q, slice(0, 8))
        below = jnp.where(z == 0, plane_ref[3, q], far)
        above = jnp.where(z == 0, far, plane_ref[0, q])
        speeds = [near_vel[f, 32 + 8 * q : 40 + 8 * q, :] for f in (0, 2, 1)]
        near_mid.append(near[q] + salt_step(near[q], below, above, around[q][0], around[q][1], speeds))
    for l in range(4):
        pair = [salt_mid_ref[l, q] for q in range(2)]
        before = pltpu.roll(jnp.where(line == 7, rim_mid[l], pair[1]), 1, 0)
        after = pltpu.roll(jnp.where(line == 0, rim_mid[l], pair[0]), 7, 0)
        around = ((before, pair[1]), (pair[0], after))
        for q in range(2):
            speeds = [vel[f, 16 * l + 8 * q : 16 * l + 8 * q + 8, :] for f in (0, 2, 1)]
            below = jnp.where(z == 1, near_mid[q], 0.0) if l == 0 else salt_mid_ref[l - 1, q]
            above = jnp.where(z == 0, near_mid[q], 0.0) if l == 3 else salt_mid_ref[l + 1, q]
            x = pair[q]
            step = salt_step(x, below, above, around[q][0], around[q][1], speeds)
            end = 0.5 * plane_ref[l, q] + 0.5 * (x + step)
            for c in range(8):
                strip[c, l, pl.ds(q, 8, stride=2), :] = end[:, 128 * c : 128 * c + 128]
        for c in range(8):
            out_ref[l, :, 128 * c : 128 * c + 128] = strip[c, l]


def unpack_kernel(x_ref, flow_ref, heat_ref):
    for lv in range(2):
        turned = jnp.concatenate([x_ref[j, lv] for j in range(16)], axis=0).T
        for f in range(3):
            flow_ref[f, lv] = turned[32 * f : 32 * f + 32]
        heat_ref[lv] = turned[96:128]


SPACES = {"h": pl.BlockSpec(memory_space=pltpu.HBM), "v": pl.BlockSpec(memory_space=pltpu.VMEM)}


def call(kernel, name, ins, outs, scratch=(), grant=16):
    return pl.pallas_call(
        kernel,
        name=name,
        in_specs=[SPACES[letter] for letter in ins],
        out_specs=[SPACES["v"] for _ in outs],
        out_shape=[jax.ShapeDtypeStruct(s, F32) for s in outs],
        scratch_shapes=list(scratch),
        compiler_params=pltpu.CompilerParams(vmem_limit_bytes=grant * 2**20),
    )


def swap(x, axes, n, start):
    pairs = []
    for i in range(start, n - 1, 2):
        pairs += [(i, i + 1), (i + 1, i)]
    return lax.ppermute(x, axes, pairs)


def on_device(flow, heat, salt):
    vmem = pltpu.VMEM
    refine = jnp.asarray(REFINE, BF16)
    refine_split = jnp.asarray(REFINE_SPLIT, BF16)
    restrict_m = jnp.asarray(RESTRICT, BF16)
    own_levels = jnp.asarray(OWN, BF16)
    all_levels = jnp.asarray(ALL, BF16)
    (a,) = call(
        turn_kernel,
        "turn",
        "hh",
        [(16, 2, 2, 8, 128)],
        [vmem((4, 2, 32, 128), F32), pltpu.SemaphoreType.DMA((2,))],
        grant=60,
    )(flow, heat)
    g, means, planes = call(
        pack_kernel, "pack", "vv", [(10, 8, NX), (2, 8, NX), (4, 2, 8, NF)], [vmem((8, 4, 16, 128), F32)]
    )(salt, restrict_m)
    g = swap(g, "gz", 2, 0)
    d = lax.all_to_all(a.reshape(32, 2, 8, 128), ("gy", "gz"), 0, 0, tiled=True)
    rims = [(13, 8, NX)] * 2
    c, near, far, _, _ = call(send_kernel, "send", "vvvv", [(5, 4, 8, NX)] + rims + rims)(
        d.reshape(16, 4, 8, 128), planes, means, g
    )
    near = swap(near, ("gx", "gy"), 128, 0)
    far = swap(far, ("gx", "gy"), 128, 1)
    fields = [(4, 8, 16, NX)] * 2
    msg, cp, mp, salt_mid, u, v = call(
        coarse_kernel,
        "coarse",
        "vvvvvvvvvv",
        [(16, 2, 8, 128)] + fields + [(4, 2, 8, NF)] + rims,
        [vmem((3, 64, NF), F32)],
    )(c, near, far, planes, g, refine, refine_split, restrict_m, own_levels, all_levels)
    back = lax.all_to_all(msg, "gy", 0, 0, tiled=True)
    (salt_end,) = call(
        salt_kernel,
        "salt",
        "vvvvvvvvv",
        [(4, 16, NF)],
        [vmem((3, 64, NF), F32), vmem((3, 48, NF), F32), vmem((8, 4, 16, 128), F32)],
    )(cp, mp, salt_mid, planes, u, v, g, refine, own_levels)
    flow_end, heat_end = call(unpack_kernel, "unpack", "v", [(3, 2, 32, 128), (2, 32, 128)])(back)
    return flow_end, heat_end, salt_end


def solution(mesh):
    specs = (P(None, "gz", "gy", "gx"), P("gz", "gy", "gx"), P("gz", ("gx", "gy"), None))
    return jax.shard_map(on_device, mesh=mesh, in_specs=specs, out_specs=specs, check_vma=False)
```

```python
import jax
import jax.numpy as jnp
import numpy as np
from jax import lax
from jax.experimental import pallas as pl
from jax.experimental.pallas import tpu as pltpu
from jax.sharding import PartitionSpec as P


F32 = jnp.float32
BF16 = jnp.bfloat16
DT = 0.1
EVEN = (-0.0390625, 0.2734375, 0.8203125, -0.0546875)
ODD = (-0.0546875, 0.8203125, 0.2734375, -0.0390625)
KINDS = (0.2, 0.2, 0.2, 0.15)
NX = 512
NF = 1024


def refine_matrix():
    matrix = np.zeros((256, 256), np.float32)
    for n in range(256):
        i = 64 + n // 2
        for k in range(4):
            matrix[i + k - (2 if n % 2 == 0 else 1), n] = (EVEN if n % 2 == 0 else ODD)[k]
    return matrix


def restrict_matrix():
    matrix = np.zeros((256, 128), np.float32)
    for n in range(256):
        matrix[n, n // 2] = 0.125
    return matrix


def level_row_matrix(levels, parts):
    rows = np.zeros((2, 16, 16), np.float64)
    for q, weights in enumerate((EVEN, ODD)):
        for i in range(16):
            for k in range(4):
                rows[q, i, (i + k - 2 + q) % 16] = weights[k]
    deep = np.zeros((len(levels), 4), np.float64)
    for n, l in enumerate(levels):
        for k in range(4):
            m = l // 2 + k - 2 + l % 2
            if 0 <= m < 4:
                deep[n, m] = (EVEN, ODD)[l % 2][k]
    whole = np.einsum("lm,qij->lqimj", deep, rows[:, :parts]).reshape(len(levels) * 2 * parts, 64)
    high = whole.astype(np.float32).astype(jnp.bfloat16).astype(np.float64)
    return np.concatenate([high, high, whole - high], axis=1).astype(np.float32)


REFINE = refine_matrix()
REFINE_SPLIT = np.concatenate([REFINE[:, 0::2], REFINE[:, 1::2]], axis=1)
RESTRICT = restrict_matrix()
OWN = np.stack([level_row_matrix(range(4 * z, 4 * z + 4), 8) for z in range(2)])
ALL = level_row_matrix(range(8), 16)


def dot(a, b):
    return jnp.dot(a, b, preferred_element_type=F32)


def split(x):
    high = x.astype(BF16)
    return high, (x - high.astype(F32)).astype(BF16)


def row(x, s):
    n = x.shape[0]
    return x if s % n == 0 else pltpu.roll(x, (-s) % n, 0)


def iota(shape, axis):
    return lax.broadcasted_iota(jnp.int32, shape, axis)


def right(x):
    n = x.shape[1]
    return jnp.where(iota(x.shape, 1) == n - 1, 0.0, pltpu.roll(x, n - 1, 1))


def left(x):
    return jnp.where(iota(x.shape, 1) == 0, 0.0, pltpu.roll(x, 1, 1))


def weigh(weights, terms):
    total = None
    for w, t in zip(weights, terms):
        if t is not None:
            total = w * t if total is None else total + w * t
    return total


def refine_rows(x, keep):
    m2, m1, p1, p2 = (row(x, s)[:keep] for s in (-2, -1, 1, 2))
    x = x[:keep]
    return weigh(EVEN, (m2, m1, x, p1)), weigh(ODD, (m1, x, p1, p2))


def turn_blocks(x):
    lane = iota((8, 128), 1)
    low = lane < 64
    even = (lane // 32) % 2 == 0
    y0 = jnp.where(low, x[0], pltpu.roll(x[2], 64, 1))
    y2 = jnp.where(low, pltpu.roll(x[0], 64, 1), x[2])
    y1 = jnp.where(low, x[1], pltpu.roll(x[3], 64, 1))
    y3 = jnp.where(low, pltpu.roll(x[1], 64, 1), x[3])
    out = []
    for a, b in ((y0, y1), (y2, y3)):
        out.append(jnp.where(even, a, pltpu.roll(b, 32, 1)))
        out.append(jnp.where(even, pltpu.roll(a, 96, 1), b))
    return out


def restrict(total, matrix):
    high, low = split(total)
    parts = []
    for b in range(4):
        window = slice(256 * b, 256 * b + 256)
        parts.append(dot(high[:, window], matrix) + dot(low[:, window], matrix))
    return jnp.concatenate(parts, axis=1)


def by_levels_rows(matrix, fields):
    high, low = split(fields.reshape(64, NX))
    return dot(matrix, jnp.concatenate([high, low, high], axis=0))


def windows(x, matrix_ref, halves):
    high, low = split(x)
    parts = []
    for b in range(-1, 4):
        w = slice(max(128 * b, 0), min(128 * b + 256, NX))
        if b == -1:
            matrix = matrix_ref[128:256, :] if halves else matrix_ref[128:256, 128:256]
        elif b == 3:
            matrix = matrix_ref[0:128, :] if halves else matrix_ref[0:128, 0:128]
        else:
            matrix = matrix_ref[...]
        parts.append(dot(jnp.concatenate([high[:, w], low[:, w]], axis=1), jnp.concatenate([matrix, matrix], axis=0)))
    return parts


def refined_rows(x, matrix_ref):
    return jnp.concatenate(windows(x, matrix_ref, False), axis=1)


def heat_mean(x, keep, matrix_ref):
    sums = []
    for t in windows(x, matrix_ref, True):
        total = 0.0
        for j in range(4):
            for h in range(2):
                piece = t[keep * j : keep * j + keep, 128 * h : 128 * h + 128]
                total = total + piece * (1.0 + 0.5 * piece)
        sums.append(pltpu.roll(total, 64, 1))
    low_half = iota((keep, 128), 1) < 64
    return 0.125 * jnp.concatenate([jnp.where(low_half, sums[c], sums[c + 1]) for c in range(4)], axis=1)


def upwind(speed, positive, below, above):
    return speed * jnp.where(positive, below, above)


def wide(ref, tile, rows):
    return jnp.concatenate([ref[tile, rows, :], ref[tile + 1, rows, :]], axis=-1)


def turn_kernel(flow_hbm, heat_hbm, a_ref, tile, sems):
    copies = [pltpu.make_async_copy(flow_hbm, tile.at[pl.ds(0, 3)], sems.at[0])]
    copies.append(pltpu.make_async_copy(heat_hbm, tile.at[3], sems.at[1]))
    for copy in copies:
        copy.start()
    for copy in copies:
        copy.wait()
    for lv in range(2):
        turned = jnp.concatenate([tile[f, lv] for f in range(4)], axis=0).T
        for j in range(16):
            piece = turned[8 * j : 8 * j + 8]
            a_ref[j, 0, lv] = piece
            a_ref[j, 1, lv] = piece


def to_sides(near_ref, far_ref, tile, up, down):
    leads = lax.rem(lax.axis_index("gy"), 2) == 0
    near_ref[tile] = jnp.where(leads, up, down)
    far_ref[tile] = jnp.where(leads, down, up)


def few_rows(a, b, c, d):
    line = iota((8, NX), 0)
    out = jnp.where(line < 2, a, pltpu.roll(b, 2, 0))
    if c is not None:
        out = jnp.where(line < 4, out, jnp.where(line == 4, c, d))
    return out


def pack_kernel(salt_ref, restrict_ref, g_ref, mean_ref, plane_ref, near_ref, far_ref, strip, up, down):
    z = lax.axis_index("gz")
    for l in range(4):
        for c in range(8):
            strip[c, l] = salt_ref[l, :, 128 * c : 128 * c + 128]
    for l in range(4):
        for q in range(2):
            for c in range(8):
                plane_ref[l, q, :, 128 * c : 128 * c + 128] = strip[c, l, pl.ds(q, 8, stride=2), :]
    totals = []
    for m in range(2):
        totals.append(sum(plane_ref[2 * m + p, q] for p in range(2) for q in range(2)))
    means = restrict(jnp.concatenate(totals, axis=0), restrict_ref[...])
    for m in range(2):
        mean_ref[m] = means[8 * m : 8 * m + 8]
        g_ref[8 + m] = means[8 * m : 8 * m + 8]
    for h in range(2):
        w = slice(512 * h, 512 * h + 512)
        for l in range(4):
            for q in range(2):
                k = 2 * l + q
                down[h, k : k + 1, :] = plane_ref[l, q, 0:1, w]
                up[h, k : k + 1, :] = plane_ref[l, q, 7:8, w]
        to_sides(near_ref, far_ref, h, up[h], down[h])
    low, high = (means[0:8], means[8:16])
    rolled = few_rows(pltpu.roll(low, 2, 0), pltpu.roll(high, 2, 0), None, None)
    to_sides(near_ref, far_ref, 2, rolled, few_rows(low, high, None, None))
    for near in range(2):
        level = jnp.where(z == 0, 3 - near, near)
        for q in range(2):
            plane = plane_ref[level, q]
            for h in range(2):
                g_ref[4 * near + 2 * q + h] = plane[:, 512 * h : 512 * h + 512]


def mean_of(mean_ref, g_ref, z, m):
    return jnp.where(z == m // 2, mean_ref[m % 2], g_ref[8 + m % 2])


def send_kernel(d_ref, mean_ref, g_ref, c_ref, near_ref, far_ref):
    z = lax.axis_index("gz")
    for m in range(4):
        for b in range(4):
            tiles = turn_blocks([d_ref[4 * b + j, m] for j in range(4)])
            for f in range(4):
                c_ref[f, m, :, 128 * b : 128 * b + 128] = tiles[f]
        c_ref[4, m] = mean_of(mean_ref, g_ref, z, m)
    first = iota((8, NX), 0) < 4
    for f in range(4):
        for p in range(2):
            a = c_ref[f, 2 * p]
            b = c_ref[f, 2 * p + 1]
            down = jnp.where(first, a, pltpu.roll(b, 4, 0))
            up = jnp.where(first, pltpu.roll(a, 4, 0), b)
            to_sides(near_ref, far_ref, 2 * f + p, up, down)
    low, high = (g_ref[8], g_ref[9])
    rows = [jnp.broadcast_to(g_ref[h, 0:1, :], (8, NX)) for h in range(2)]
    down = few_rows(low, high, rows[0], rows[1])
    rows = [jnp.broadcast_to(g_ref[2 + h, 7:8, :], (8, NX)) for h in range(2)]
    up = few_rows(pltpu.roll(low, 2, 0), pltpu.roll(high, 2, 0), rows[0], rows[1])
    to_sides(near_ref, far_ref, 8, up, down)


def coarse_rate(q, below, above, speeds, positives, diffusion, keep):
    x = q[:keep]
    up = (above - x, right(x) - x, row(q, 1)[:keep] - x)
    down = (x - below, x - left(x), x - row(q, -1)[:keep])
    spread = (up[0] - down[0]) + (up[1] - down[1]) + (up[2] - down[2])
    carried = sum(upwind(a, s, d, u) for a, s, d, u in zip(speeds, positives, down, up))
    return diffusion * spread - carried


def salt_step(x, below, above, before, after, speeds):
    up = (above - x, after - x, right(x) - x)
    down = (x - below, x - before, x - left(x))
    spread = (up[0] - down[0]) + (up[1] - down[1]) + (up[2] - down[2])
    carried = sum(upwind(a, a > 0, d, u) for a, d, u in zip(speeds, down, up))
    return (DT * 0.05 / 0.25) * spread - (DT / 0.5) * carried


def edge_row(ref, k):
    whole = jnp.concatenate([ref[9, k : k + 1, :], ref[10, k : k + 1, :]], axis=-1)
    return jnp.broadcast_to(whole, (8, NF))


def near_edge(ref):
    whole = jnp.concatenate([ref[8, 4:5, :], ref[8, 5:6, :]], axis=-1)
    return jnp.broadcast_to(whole, (8, NF))


def levels_of(fields, f, start, parity):
    return weigh(EVEN if parity == 0 else ODD, [fields[f, start + parity + k] for k in range(4)])


def rim_of(ur_ref, dr_ref, f, m):
    first = iota((8, NX), 0) < 4
    d = dr_ref[2 * f + m // 2]
    u = ur_ref[2 * f + m // 2]
    if m % 2 == 0:
        return jnp.where(first, d, pltpu.roll(u, 4, 0))
    return jnp.where(first, pltpu.roll(d, 4, 0), u)


def coarse_kernel(
    c_ref, near_ref, far_ref, near_salt_ref, far_salt_ref, plane_ref, g_ref, refine_ref, refine_split_ref, restrict_ref, own_ref, all_ref,
    msg_ref, cp, mp, salt_mid, ur_ref, dr_ref, vel,
):
    z = lax.axis_index("gz")
    leads = lax.rem(lax.axis_index("gy"), 2) == 0
    place = lax.axis_index("gx") * 16 + lax.axis_index("gy")
    for t in range(12):
        near = near_ref[t] if t < 9 else near_salt_ref[t - 9]
        far = far_ref[t] if t < 9 else far_salt_ref[t - 9]
        ur_ref[t] = jnp.where(leads, far, near)
        dr_ref[t] = jnp.where(leads, near, far)
    zero = jnp.zeros((16, NX), F32)
    for f in range(4):
        for k in (0, 1, 6, 7):
            cp[f, k] = zero
            mp[f, k] = zero
        for m in range(4):
            cp[f, m + 2, 0:8, :] = c_ref[f, m]
            cp[f, m + 2, 8:16, :] = rim_of(ur_ref, dr_ref, f, m)
    own_matrix = own_ref[z]
    for f in range(3):
        vel[f] = refined_rows(by_levels_rows(own_matrix, cp[f, 2:6]), refine_ref)
    rows16 = iota((16, NX), 0)
    inside = ((rows16 < 8) | (rows16 >= 12) | (place != 127)) & ((rows16 < 12) | (place != 0))
    heat = by_levels_rows(all_ref[...], cp[3, 2:6])
    for m in range(4):
        own_level = z == m // 2
        below = jnp.where(own_level, dr_ref[11], dr_ref[8])
        above = jnp.where(own_level, ur_ref[11], ur_ref[8])
        if m % 2 == 1:
            below = pltpu.roll(below, 6, 0)
            above = pltpu.roll(above, 4, 0)
        else:
            above = pltpu.roll(above, 6, 0)
        rim = jnp.where(iota((8, NX), 0) < 2, below, above)
        salt_mean = jnp.concatenate([c_ref[4, m], rim], axis=0)
        buoyancy = heat_mean(heat[64 * m : 64 * m + 64], 16, refine_split_ref) - 0.8 * salt_mean
        speeds = [cp[f, m + 2] for f in range(3)]
        positives = [s > 0 for s in speeds]
        for f in range(4):
            q = cp[f, m + 2]
            rate = coarse_rate(q, cp[f, m + 1], cp[f, m + 3], speeds, positives, KINDS[f], 16)
            if f == 0:
                rate = rate + buoyancy
            mp[f, m + 2] = jnp.where(inside, q + DT * rate, 0.0)
    line = iota((8, NF), 0)
    totals = []
    for m in range(2):
        total = None
        for p in range(2):
            l = 2 * m + p
            own = [plane_ref[l, q] for q in range(2)]
            following = jnp.where(line == 7, edge_row(dr_ref, 2 * l), pltpu.roll(own[0], 7, 0))
            preceding = jnp.where(line == 0, edge_row(ur_ref, 2 * l + 1), pltpu.roll(own[1], 1, 0))
            around = ((preceding, own[1]), (own[0], following))
            for q in range(2):
                near = wide(g_ref, 2 * q, slice(0, 8))
                below = jnp.where(z == 1, near, 0.0) if l == 0 else plane_ref[l - 1, q]
                above = jnp.where(z == 0, near, 0.0) if l == 3 else plane_ref[l + 1, q]
                speeds = [vel[f, 16 * l + 8 * q : 16 * l + 8 * q + 8, :] for f in (0, 2, 1)]
                x = own[q]
                mid = x + salt_step(x, below, above, around[q][0], around[q][1], speeds)
                salt_mid[l, q] = mid
                total = mid if total is None else total + mid
        totals.append(total)
    means = restrict(jnp.concatenate(totals, axis=0), restrict_ref[...])
    heat = by_levels_rows(own_matrix, mp[3, 2:6])
    for m in range(2):
        buoyancy = heat_mean(heat[32 * m : 32 * m + 32], 8, refine_split_ref) - 0.8 * means[8 * m : 8 * m + 8]
        at = 2 * z + m + 2
        speeds = [mp[f, at, 0:8, :] for f in range(3)]
        positives = [s > 0 for s in speeds]
        ends = []
        for f in range(4):
            q = mp[f, at]
            rate = coarse_rate(q, mp[f, at - 1, 0:8, :], mp[f, at + 1, 0:8, :], speeds, positives, KINDS[f], 8)
            if f == 0:
                rate = rate + buoyancy
            ends.append(0.5 * cp[f, at, 0:8, :] + 0.5 * (q[:8] + DT * rate))
        for b in range(4):
            tiles = turn_blocks([ends[f][:, 128 * b : 128 * b + 128] for f in range(4)])
            for j in range(4):
                msg_ref[4 * b + j, m] = tiles[j]


def salt_kernel(
    cp, mv, salt_mid_ref, plane_ref, ur_ref, dr_ref, g_ref, refine_ref, own_ref, out_ref, vel, near_vel, strip,
):
    z = lax.axis_index("gz")
    place = lax.axis_index("gx") * 16 + lax.axis_index("gy")
    top = iota((8, NX), 0) == 0
    for f in range(3):
        rims = []
        for m in range(2):
            for p in range(2):
                even, odd = refine_rows(levels_of(cp, f, 2 * z + m, p), 16)
                rims.append(jnp.where(top, even[8:], odd[8:]))
        weights = [jnp.where(z == 0, EVEN[k], ODD[k]) for k in range(4)]
        rims.extend(refine_rows(weigh(weights, [cp[f, 2 + k] for k in range(4)]), 8))
        near_vel[f] = refined_rows(jnp.concatenate(rims, axis=0), refine_ref)
    for f in range(3):
        vel[f] = refined_rows(by_levels_rows(own_ref[z], mv[f, 2:6]), refine_ref)
    line = iota((8, NF), 0)
    rim = [jnp.where(line == 0, edge_row(dr_ref, 2 * l), edge_row(ur_ref, 2 * l + 1)) for l in range(4)]
    near_rim = jnp.where(line == 0, near_edge(dr_ref), near_edge(ur_ref))
    bottom = jnp.where(z == 1, near_rim, 0.0)
    roof = jnp.where(z == 0, near_rim, 0.0)
    alive = ((line != 0) | (place != 127)) & ((line != 7) | (place != 0))
    rim_mid = []
    for l in range(4):
        before = jnp.where(line == 0, pltpu.roll(plane_ref[l, 1], 1, 0), edge_row(ur_ref, 2 * l))
        after = jnp.where(line == 0, edge_row(dr_ref, 2 * l + 1), pltpu.roll(plane_ref[l, 0], 7, 0))
        speeds = [near_vel[f, 8 * l : 8 * l + 8, :] for f in (0, 2, 1)]
        below = bottom if l == 0 else rim[l - 1]
        above = roof if l == 3 else rim[l + 1]
        mid = rim[l] + salt_step(rim[l], below, above, before, after, speeds)
        rim_mid.append(jnp.where(alive, mid, 0.0))
    near = [wide(g_ref, 2 * q, slice(0, 8)) for q in range(2)]
    before = jnp.where(line == 0, near_edge(ur_ref), pltpu.roll(near[1], 1, 0))
    after = jnp.where(line == 7, near_edge(dr_ref), pltpu.roll(near[0], 7, 0))
    around = ((before, near[1]), (near[0], after))
    near_mid = []
    for q in range(2):
        far = wide(g_ref, 4 + 2 * q, slice(0, 8))
        below = jnp.where(z == 0, plane_ref[3, q], far)
        above = jnp.where(z == 0, far, plane_ref[0, q])
        speeds = [near_vel[f, 32 + 8 * q : 40 + 8 * q, :] for f in (0, 2, 1)]
        near_mid.append(near[q] + salt_step(near[q], below, above, around[q][0], around[q][1], speeds))
    for l in range(4):
        pair = [salt_mid_ref[l, q] for q in range(2)]
        before = pltpu.roll(jnp.where(line == 7, rim_mid[l], pair[1]), 1, 0)
        after = pltpu.roll(jnp.where(line == 0, rim_mid[l], pair[0]), 7, 0)
        around = ((before, pair[1]), (pair[0], after))
        for q in range(2):
            speeds = [vel[f, 16 * l + 8 * q : 16 * l + 8 * q + 8, :] for f in (0, 2, 1)]
            below = jnp.where(z == 1, near_mid[q], 0.0) if l == 0 else salt_mid_ref[l - 1, q]
            above = jnp.where(z == 0, near_mid[q], 0.0) if l == 3 else salt_mid_ref[l + 1, q]
            x = pair[q]
            step = salt_step(x, below, above, around[q][0], around[q][1], speeds)
            end = 0.5 * plane_ref[l, q] + 0.5 * (x + step)
            for c in range(8):
                strip[c, l, pl.ds(q, 8, stride=2), :] = end[:, 128 * c : 128 * c + 128]
        for c in range(8):
            out_ref[l, :, 128 * c : 128 * c + 128] = strip[c, l]


def unpack_kernel(x_ref, flow_ref, heat_ref):
    for lv in range(2):
        turned = jnp.concatenate([x_ref[j, lv] for j in range(16)], axis=0).T
        for f in range(3):
            flow_ref[f, lv] = turned[32 * f : 32 * f + 32]
        heat_ref[lv] = turned[96:128]


SPACES = {"h": pl.BlockSpec(memory_space=pltpu.HBM), "v": pl.BlockSpec(memory_space=pltpu.VMEM)}


def call(kernel, ins, outs, scratch=(), grant=16):
    return pl.pallas_call(
        kernel,
        in_specs=[SPACES[letter] for letter in ins],
        out_specs=[SPACES["v"] for _ in outs],
        out_shape=[jax.ShapeDtypeStruct(s, F32) for s in outs],
        scratch_shapes=list(scratch),
        compiler_params=pltpu.CompilerParams(vmem_limit_bytes=grant * 2**20),
    )


def swap(x, axes, n, start):
    pairs = []
    for i in range(start, n - 1, 2):
        pairs += [(i, i + 1), (i + 1, i)]
    return lax.ppermute(x, axes, pairs)


def step(flow, heat, salt):
    vmem = pltpu.VMEM
    refine = jnp.asarray(REFINE, BF16)
    refine_split = jnp.asarray(REFINE_SPLIT, BF16)
    restrict_m = jnp.asarray(RESTRICT, BF16)
    own_levels = jnp.asarray(OWN, BF16)
    all_levels = jnp.asarray(ALL, BF16)
    (a,) = call(
        turn_kernel, "hh", [(16, 2, 2, 8, 128)], [vmem((4, 2, 32, 128), F32), pltpu.SemaphoreType.DMA((2,))], grant=60
    )(flow, heat)
    g, means, planes, near_salt, far_salt = call(
        pack_kernel,
        "vv",
        [(10, 8, NX), (2, 8, NX), (4, 2, 8, NF), (3, 8, NX), (3, 8, NX)],
        [vmem((8, 4, 16, 128), F32), vmem((2, 8, NX), F32), vmem((2, 8, NX), F32)],
    )(salt, restrict_m)
    g = swap(g, "gz", 2, 0)
    near_salt = swap(near_salt, ("gx", "gy"), 128, 0)
    far_salt = swap(far_salt, ("gx", "gy"), 128, 1)
    d = lax.all_to_all(a.reshape(32, 2, 8, 128), ("gy", "gz"), 0, 0, tiled=True)
    c, near, far = call(send_kernel, "vvv", [(5, 4, 8, NX), (9, 8, NX), (9, 8, NX)])(d.reshape(16, 4, 8, 128), means, g)
    near = swap(near, ("gx", "gy"), 128, 0)
    far = swap(far, ("gx", "gy"), 128, 1)
    rims = [(12, 8, NX)] * 2
    fields = [(4, 8, 16, NX)] * 2
    msg, cp, mp, salt_mid, u, v = call(
        coarse_kernel, "vvvvvvvvvvvv", [(16, 2, 8, 128)] + fields + [(4, 2, 8, NF)] + rims, [vmem((3, 64, NF), F32)]
    )(c, near, far, near_salt, far_salt, planes, g, refine, refine_split, restrict_m, own_levels, all_levels)
    back = lax.all_to_all(msg, "gy", 0, 0, tiled=True)
    (salt_end,) = call(
        salt_kernel,
        "vvvvvvvvv",
        [(4, 16, NF)],
        [vmem((3, 64, NF), F32), vmem((3, 48, NF), F32), vmem((8, 4, 16, 128), F32)],
    )(cp, mp, salt_mid, planes, u, v, g, refine, own_levels)
    flow_end, heat_end = call(unpack_kernel, "v", [(3, 2, 32, 128), (2, 32, 128)])(back)
    return flow_end, heat_end, salt_end


def solution(mesh):
    specs = (P(None, "gz", "gy", "gx"), P("gz", "gy", "gx"), P("gz", ("gx", "gy"), None))
    return jax.shard_map(step, mesh=mesh, in_specs=specs, out_specs=specs, check_vma=False)
```

```python
import jax
import jax.numpy as jnp
import numpy as np
from jax import lax
from jax.experimental import pallas as pl
from jax.experimental.pallas import tpu as pltpu
from jax.sharding import PartitionSpec as P


F32 = jnp.float32
BF16 = jnp.bfloat16
DT = 0.1
EVEN = (-0.0390625, 0.2734375, 0.8203125, -0.0546875)
ODD = (-0.0546875, 0.8203125, 0.2734375, -0.0390625)
KINDS = (0.2, 0.2, 0.2, 0.15)
NX = 512
NF = 1024


def refine_matrix():
    matrix = np.zeros((256, 256), np.float32)
    for n in range(256):
        i = 64 + n // 2
        for k in range(4):
            matrix[i + k - (2 if n % 2 == 0 else 1), n] = (EVEN if n % 2 == 0 else ODD)[k]
    return matrix


def restrict_matrix():
    matrix = np.zeros((256, 128), np.float32)
    for n in range(256):
        matrix[n, n // 2] = 0.125
    return matrix


def level_row_matrix(levels, parts):
    rows = np.zeros((2, 16, 16), np.float64)
    for q, weights in enumerate((EVEN, ODD)):
        for i in range(16):
            for k in range(4):
                rows[q, i, (i + k - 2 + q) % 16] = weights[k]
    deep = np.zeros((len(levels), 4), np.float64)
    for n, l in enumerate(levels):
        for k in range(4):
            m = l // 2 + k - 2 + l % 2
            if 0 <= m < 4:
                deep[n, m] = (EVEN, ODD)[l % 2][k]
    whole = np.einsum("lm,qij->lqimj", deep, rows[:, :parts]).reshape(len(levels) * 2 * parts, 64)
    high = whole.astype(np.float32).astype(jnp.bfloat16).astype(np.float64)
    return np.concatenate([high, high, whole - high], axis=1).astype(np.float32)


REFINE = refine_matrix()
REFINE_SPLIT = np.concatenate([REFINE[:, 0::2], REFINE[:, 1::2]], axis=1)
RESTRICT = restrict_matrix()
OWN = np.stack([level_row_matrix(range(4 * z, 4 * z + 4), 8) for z in range(2)])
ALL = level_row_matrix(range(8), 16)


def dot(a, b):
    return jnp.dot(a, b, preferred_element_type=F32)


def split(x):
    high = x.astype(BF16)
    return high, (x - high.astype(F32)).astype(BF16)


def row(x, s):
    n = x.shape[0]
    return x if s % n == 0 else pltpu.roll(x, (-s) % n, 0)


def iota(shape, axis):
    return lax.broadcasted_iota(jnp.int32, shape, axis)


def right(x):
    n = x.shape[1] // 128
    turned = [pltpu.roll(x[:, 128 * c : 128 * c + 128], 127, 1) for c in range(n)]
    edge = iota(turned[0].shape, 1) == 127
    return jnp.concatenate([jnp.where(edge, turned[c + 1] if c < n - 1 else 0.0, turned[c]) for c in range(n)], axis=1)


def left(x):
    n = x.shape[1] // 128
    turned = [pltpu.roll(x[:, 128 * c : 128 * c + 128], 1, 1) for c in range(n)]
    edge = iota(turned[0].shape, 1) == 0
    return jnp.concatenate([jnp.where(edge, turned[c - 1] if c else 0.0, turned[c]) for c in range(n)], axis=1)


def weigh(weights, terms):
    total = None
    for w, t in zip(weights, terms):
        if t is not None:
            total = w * t if total is None else total + w * t
    return total


def refine_rows(x, keep):
    m2, m1, p1, p2 = (row(x, s)[:keep] for s in (-2, -1, 1, 2))
    x = x[:keep]
    return weigh(EVEN, (m2, m1, x, p1)), weigh(ODD, (m1, x, p1, p2))


def turn_blocks(x):
    lane = iota((8, 128), 1)
    low = lane < 64
    even = (lane // 32) % 2 == 0
    y0 = jnp.where(low, x[0], pltpu.roll(x[2], 64, 1))
    y2 = jnp.where(low, pltpu.roll(x[0], 64, 1), x[2])
    y1 = jnp.where(low, x[1], pltpu.roll(x[3], 64, 1))
    y3 = jnp.where(low, pltpu.roll(x[1], 64, 1), x[3])
    out = []
    for a, b in ((y0, y1), (y2, y3)):
        out.append(jnp.where(even, a, pltpu.roll(b, 32, 1)))
        out.append(jnp.where(even, pltpu.roll(a, 96, 1), b))
    return out


def restrict(total, matrix):
    high, low = split(total)
    parts = []
    for b in range(4):
        window = slice(256 * b, 256 * b + 256)
        parts.append(dot(high[:, window], matrix) + dot(low[:, window], matrix))
    return jnp.concatenate(parts, axis=1)


def by_levels_rows(matrix, fields):
    high, low = split(fields.reshape(64, NX))
    return dot(matrix, jnp.concatenate([high, low, high], axis=0))


def windows(x, matrix_ref, halves):
    high, low = split(x)
    parts = []
    for b in range(-1, 4):
        w = slice(max(128 * b, 0), min(128 * b + 256, NX))
        if b == -1:
            matrix = matrix_ref[128:256, :] if halves else matrix_ref[128:256, 128:256]
        elif b == 3:
            matrix = matrix_ref[0:128, :] if halves else matrix_ref[0:128, 0:128]
        else:
            matrix = matrix_ref[...]
        parts.append(dot(jnp.concatenate([high[:, w], low[:, w]], axis=1), jnp.concatenate([matrix, matrix], axis=0)))
    return parts


def refined_rows(x, matrix_ref):
    return jnp.concatenate(windows(x, matrix_ref, False), axis=1)


def heat_mean(x, keep, matrix_ref):
    sums = []
    for t in windows(x, matrix_ref, True):
        pieces = [t[keep * j : keep * j + keep, 128 * h : 128 * h + 128] for j in range(4) for h in range(2)]
        total = sum(pieces[1:], pieces[0]) + 0.5 * sum((p * p for p in pieces[1:]), pieces[0] * pieces[0])
        sums.append(pltpu.roll(total, 64, 1))
    low_half = iota((keep, 128), 1) < 64
    return 0.125 * jnp.concatenate([jnp.where(low_half, sums[c], sums[c + 1]) for c in range(4)], axis=1)


def upwind(speed, positive, below, above):
    return speed * jnp.where(positive, below, above)


def wide(ref, tile, rows):
    return jnp.concatenate([ref[tile, rows, :], ref[tile + 1, rows, :]], axis=-1)


def turn_kernel(flow_hbm, heat_hbm, a_ref, tile, sems):
    copies = [pltpu.make_async_copy(flow_hbm, tile.at[pl.ds(0, 3)], sems.at[0])]
    copies.append(pltpu.make_async_copy(heat_hbm, tile.at[3], sems.at[1]))
    for copy in copies:
        copy.start()
    for copy in copies:
        copy.wait()
    for lv in range(2):
        turned = jnp.concatenate([tile[f, lv] for f in range(4)], axis=0).T
        for j in range(16):
            piece = turned[8 * j : 8 * j + 8]
            a_ref[j, 0, lv] = piece
            a_ref[j, 1, lv] = piece


def to_sides(near_ref, far_ref, tile, up, down):
    leads = lax.rem(lax.axis_index("gy"), 2) == 0
    near_ref[tile] = jnp.where(leads, up, down)
    far_ref[tile] = jnp.where(leads, down, up)


def few_rows(a, b, c, d):
    line = iota((8, NX), 0)
    out = jnp.where(line < 2, a, pltpu.roll(b, 2, 0))
    if c is not None:
        out = jnp.where(line < 4, out, jnp.where(line == 4, c, d))
    return out


def pack_kernel(salt_ref, restrict_ref, g_ref, mean_ref, plane_ref, near_ref, far_ref, strip, up, down):
    z = lax.axis_index("gz")
    for l in range(4):
        for c in range(8):
            strip[c, l] = salt_ref[l, :, 128 * c : 128 * c + 128]
    for l in range(4):
        for q in range(2):
            for c in range(8):
                plane_ref[l, q, :, 128 * c : 128 * c + 128] = strip[c, l, pl.ds(q, 8, stride=2), :]
    totals = []
    for m in range(2):
        totals.append(sum(plane_ref[2 * m + p, q] for p in range(2) for q in range(2)))
    means = restrict(jnp.concatenate(totals, axis=0), restrict_ref[...])
    for m in range(2):
        mean_ref[m] = means[8 * m : 8 * m + 8]
        g_ref[8 + m] = means[8 * m : 8 * m + 8]
    for h in range(2):
        w = slice(512 * h, 512 * h + 512)
        for l in range(4):
            for q in range(2):
                k = 2 * l + q
                down[h, k : k + 1, :] = plane_ref[l, q, 0:1, w]
                up[h, k : k + 1, :] = plane_ref[l, q, 7:8, w]
        to_sides(near_ref, far_ref, h, up[h], down[h])
    low, high = (means[0:8], means[8:16])
    rolled = few_rows(pltpu.roll(low, 2, 0), pltpu.roll(high, 2, 0), None, None)
    to_sides(near_ref, far_ref, 2, rolled, few_rows(low, high, None, None))
    for near in range(2):
        level = jnp.where(z == 0, 3 - near, near)
        for q in range(2):
            plane = plane_ref[level, q]
            for h in range(2):
                g_ref[4 * near + 2 * q + h] = plane[:, 512 * h : 512 * h + 512]


def mean_of(mean_ref, g_ref, z, m):
    return jnp.where(z == m // 2, mean_ref[m % 2], g_ref[8 + m % 2])


def send_kernel(d_ref, mean_ref, g_ref, c_ref, near_ref, far_ref):
    z = lax.axis_index("gz")
    for m in range(4):
        for b in range(4):
            tiles = turn_blocks([d_ref[4 * b + j, m] for j in range(4)])
            for f in range(4):
                c_ref[f, m, :, 128 * b : 128 * b + 128] = tiles[f]
        c_ref[4, m] = mean_of(mean_ref, g_ref, z, m)
    first = iota((8, NX), 0) < 4
    for f in range(4):
        for p in range(2):
            a = c_ref[f, 2 * p]
            b = c_ref[f, 2 * p + 1]
            down = jnp.where(first, a, pltpu.roll(b, 4, 0))
            up = jnp.where(first, pltpu.roll(a, 4, 0), b)
            to_sides(near_ref, far_ref, 2 * f + p, up, down)
    low, high = (g_ref[8], g_ref[9])
    rows = [jnp.broadcast_to(g_ref[h, 0:1, :], (8, NX)) for h in range(2)]
    down = few_rows(low, high, rows[0], rows[1])
    rows = [jnp.broadcast_to(g_ref[2 + h, 7:8, :], (8, NX)) for h in range(2)]
    up = few_rows(pltpu.roll(low, 2, 0), pltpu.roll(high, 2, 0), rows[0], rows[1])
    to_sides(near_ref, far_ref, 8, up, down)


def winds(speeds):
    sizes = [DT * jnp.abs(a) for a in speeds]
    total = sizes[0] + sizes[1] + sizes[2]
    rests = {k: (1.0 - 6.0 * DT * k) - total for k in set(KINDS)}
    return [a > 0 for a in speeds], sizes, rests


def coarse_step(q, below, above, shared, diffusion, keep):
    positives, sizes, rests = shared
    x = q[:keep]
    after = (above, right(x), row(q, 1)[:keep])
    before = (below, left(x), row(q, -1)[:keep])
    around = ((after[0] + before[0]) + (after[1] + before[1])) + (after[2] + before[2])
    total = x * rests[diffusion] + (DT * diffusion) * around
    for positive, size, b, a in zip(positives, sizes, before, after):
        total = total + size * jnp.where(positive, b, a)
    return total


def salt_step(x, below, above, before, after, speeds):
    up = (above - x, after - x, right(x) - x)
    down = (x - below, x - before, x - left(x))
    spread = (up[0] - down[0]) + (up[1] - down[1]) + (up[2] - down[2])
    carried = sum(upwind(a, a > 0, d, u) for a, d, u in zip(speeds, down, up))
    return (DT * 0.05 / 0.25) * spread - (DT / 0.5) * carried


def edge_row(ref, k):
    whole = jnp.concatenate([ref[9, k : k + 1, :], ref[10, k : k + 1, :]], axis=-1)
    return jnp.broadcast_to(whole, (8, NF))


def near_edge(ref):
    whole = jnp.concatenate([ref[8, 4:5, :], ref[8, 5:6, :]], axis=-1)
    return jnp.broadcast_to(whole, (8, NF))


def levels_of(fields, f, start, parity):
    return weigh(EVEN if parity == 0 else ODD, [fields[f, start + parity + k] for k in range(4)])


def rim_of(ur_ref, dr_ref, f, m):
    first = iota((8, NX), 0) < 4
    d = dr_ref[2 * f + m // 2]
    u = ur_ref[2 * f + m // 2]
    if m % 2 == 0:
        return jnp.where(first, d, pltpu.roll(u, 4, 0))
    return jnp.where(first, pltpu.roll(d, 4, 0), u)


def coarse_kernel(
    c_ref, near_ref, far_ref, near_salt_ref, far_salt_ref, plane_ref, g_ref, refine_ref, refine_split_ref, restrict_ref, own_ref, all_ref,
    msg_ref, cp, mp, salt_mid, ur_ref, dr_ref, vel,
):
    z = lax.axis_index("gz")
    leads = lax.rem(lax.axis_index("gy"), 2) == 0
    place = lax.axis_index("gx") * 16 + lax.axis_index("gy")
    for t in range(12):
        near = near_ref[t] if t < 9 else near_salt_ref[t - 9]
        far = far_ref[t] if t < 9 else far_salt_ref[t - 9]
        ur_ref[t] = jnp.where(leads, far, near)
        dr_ref[t] = jnp.where(leads, near, far)
    zero = jnp.zeros((16, NX), F32)
    for f in range(4):
        for k in (0, 1, 6, 7):
            cp[f, k] = zero
            mp[f, k] = zero
        for m in range(4):
            cp[f, m + 2, 0:8, :] = c_ref[f, m]
            cp[f, m + 2, 8:16, :] = rim_of(ur_ref, dr_ref, f, m)
    own_matrix = own_ref[z]
    heat = by_levels_rows(all_ref[...], cp[3, 2:6])
    winding = [by_levels_rows(own_matrix, cp[f, 2:6]) for f in range(3)]
    rows16 = iota((16, NX), 0)
    inside = ((rows16 < 8) | (rows16 >= 12) | (place != 127)) & ((rows16 < 12) | (place != 0))
    two = iota((8, NX), 0) < 2
    for m in range(4):
        shared = winds([cp[f, m + 2] for f in range(3)])
        for f in (3, 1, 2, 0):
            mid = coarse_step(cp[f, m + 2], cp[f, m + 1], cp[f, m + 3], shared, KINDS[f], 16)
            if f == 0:
                own_level = z == m // 2
                below = jnp.where(own_level, dr_ref[11], dr_ref[8])
                above = jnp.where(own_level, ur_ref[11], ur_ref[8])
                if m % 2 == 1:
                    below = pltpu.roll(below, 6, 0)
                    above = pltpu.roll(above, 4, 0)
                else:
                    above = pltpu.roll(above, 6, 0)
                salt_mean = jnp.concatenate([c_ref[4, m], jnp.where(two, below, above)], axis=0)
                buoyancy = heat_mean(heat[64 * m : 64 * m + 64], 16, refine_split_ref) - 0.8 * salt_mean
                mid = mid + DT * buoyancy
            mp[f, m + 2] = jnp.where(inside, mid, 0.0)
        if m < 3:
            vel[m] = refined_rows(winding[m], refine_ref)
    heat = by_levels_rows(own_matrix, mp[3, 2:6])
    line = iota((8, NF), 0)
    totals = []
    heats = []
    for m in range(2):
        heats.append(heat_mean(heat[32 * m : 32 * m + 32], 8, refine_split_ref))
        total = None
        for p in range(2):
            l = 2 * m + p
            own = [plane_ref[l, q] for q in range(2)]
            following = jnp.where(line == 7, edge_row(dr_ref, 2 * l), pltpu.roll(own[0], 7, 0))
            preceding = jnp.where(line == 0, edge_row(ur_ref, 2 * l + 1), pltpu.roll(own[1], 1, 0))
            around = ((preceding, own[1]), (own[0], following))
            for q in range(2):
                near = wide(g_ref, 2 * q, slice(0, 8))
                below = jnp.where(z == 1, near, 0.0) if l == 0 else plane_ref[l - 1, q]
                above = jnp.where(z == 0, near, 0.0) if l == 3 else plane_ref[l + 1, q]
                speeds = [vel[f, 16 * l + 8 * q : 16 * l + 8 * q + 8, :] for f in (0, 2, 1)]
                x = own[q]
                mid = x + salt_step(x, below, above, around[q][0], around[q][1], speeds)
                salt_mid[l, q] = mid
                total = mid if total is None else total + mid
        totals.append(total)
    means = restrict(jnp.concatenate(totals, axis=0), restrict_ref[...])
    for m in range(2):
        at = 2 * z + m + 2
        shared = winds([mp[f, at, 0:8, :] for f in range(3)])
        ends = []
        for f in (1, 2, 3, 0):
            end = coarse_step(mp[f, at], mp[f, at - 1, 0:8, :], mp[f, at + 1, 0:8, :], shared, KINDS[f], 8)
            if f == 0:
                end = end + DT * (heats[m] - 0.8 * means[8 * m : 8 * m + 8])
            ends.append(0.5 * cp[f, at, 0:8, :] + 0.5 * end)
        ends = ends[3:] + ends[:3]
        for b in range(4):
            tiles = turn_blocks([ends[f][:, 128 * b : 128 * b + 128] for f in range(4)])
            for j in range(4):
                msg_ref[4 * b + j, m] = tiles[j]


def salt_kernel(
    cp, mv, salt_mid_ref, plane_ref, ur_ref, dr_ref, g_ref, refine_ref, own_ref, out_ref, vel, near_vel, strip,
):
    z = lax.axis_index("gz")
    place = lax.axis_index("gx") * 16 + lax.axis_index("gy")
    top = iota((8, NX), 0) == 0
    for f in range(3):
        rims = []
        for m in range(2):
            for p in range(2):
                even, odd = refine_rows(levels_of(cp, f, 2 * z + m, p), 16)
                rims.append(jnp.where(top, even[8:], odd[8:]))
        weights = [jnp.where(z == 0, EVEN[k], ODD[k]) for k in range(4)]
        rims.extend(refine_rows(weigh(weights, [cp[f, 2 + k] for k in range(4)]), 8))
        near_vel[f] = refined_rows(jnp.concatenate(rims, axis=0), refine_ref)
    for f in range(3):
        vel[f] = refined_rows(by_levels_rows(own_ref[z], mv[f, 2:6]), refine_ref)
    line = iota((8, NF), 0)
    rim = [jnp.where(line == 0, edge_row(dr_ref, 2 * l), edge_row(ur_ref, 2 * l + 1)) for l in range(4)]
    near_rim = jnp.where(line == 0, near_edge(dr_ref), near_edge(ur_ref))
    bottom = jnp.where(z == 1, near_rim, 0.0)
    roof = jnp.where(z == 0, near_rim, 0.0)
    alive = ((line != 0) | (place != 127)) & ((line != 7) | (place != 0))
    rim_mid = []
    for l in range(4):
        before = jnp.where(line == 0, pltpu.roll(plane_ref[l, 1], 1, 0), edge_row(ur_ref, 2 * l))
        after = jnp.where(line == 0, edge_row(dr_ref, 2 * l + 1), pltpu.roll(plane_ref[l, 0], 7, 0))
        speeds = [near_vel[f, 8 * l : 8 * l + 8, :] for f in (0, 2, 1)]
        below = bottom if l == 0 else rim[l - 1]
        above = roof if l == 3 else rim[l + 1]
        mid = rim[l] + salt_step(rim[l], below, above, before, after, speeds)
        rim_mid.append(jnp.where(alive, mid, 0.0))
    near = [wide(g_ref, 2 * q, slice(0, 8)) for q in range(2)]
    before = jnp.where(line == 0, near_edge(ur_ref), pltpu.roll(near[1], 1, 0))
    after = jnp.where(line == 7, near_edge(dr_ref), pltpu.roll(near[0], 7, 0))
    around = ((before, near[1]), (near[0], after))
    near_mid = []
    for q in range(2):
        far = wide(g_ref, 4 + 2 * q, slice(0, 8))
        below = jnp.where(z == 0, plane_ref[3, q], far)
        above = jnp.where(z == 0, far, plane_ref[0, q])
        speeds = [near_vel[f, 32 + 8 * q : 40 + 8 * q, :] for f in (0, 2, 1)]
        near_mid.append(near[q] + salt_step(near[q], below, above, around[q][0], around[q][1], speeds))
    for l in range(4):
        pair = [salt_mid_ref[l, q] for q in range(2)]
        before = pltpu.roll(jnp.where(line == 7, rim_mid[l], pair[1]), 1, 0)
        after = pltpu.roll(jnp.where(line == 0, rim_mid[l], pair[0]), 7, 0)
        around = ((before, pair[1]), (pair[0], after))
        for q in range(2):
            speeds = [vel[f, 16 * l + 8 * q : 16 * l + 8 * q + 8, :] for f in (0, 2, 1)]
            below = jnp.where(z == 1, near_mid[q], 0.0) if l == 0 else salt_mid_ref[l - 1, q]
            above = jnp.where(z == 0, near_mid[q], 0.0) if l == 3 else salt_mid_ref[l + 1, q]
            x = pair[q]
            step = salt_step(x, below, above, around[q][0], around[q][1], speeds)
            end = 0.5 * plane_ref[l, q] + 0.5 * (x + step)
            for c in range(8):
                strip[c, l, pl.ds(q, 8, stride=2), :] = end[:, 128 * c : 128 * c + 128]
        for c in range(8):
            out_ref[l, :, 128 * c : 128 * c + 128] = strip[c, l]


def unpack_kernel(x_ref, flow_ref, heat_ref):
    for lv in range(2):
        turned = jnp.concatenate([x_ref[j, lv] for j in range(16)], axis=0).T
        for f in range(3):
            flow_ref[f, lv] = turned[32 * f : 32 * f + 32]
        heat_ref[lv] = turned[96:128]


SPACES = {"h": pl.BlockSpec(memory_space=pltpu.HBM), "v": pl.BlockSpec(memory_space=pltpu.VMEM)}


def call(kernel, ins, outs, scratch=(), grant=16):
    return pl.pallas_call(
        kernel,
        in_specs=[SPACES[letter] for letter in ins],
        out_specs=[SPACES["v"] for _ in outs],
        out_shape=[jax.ShapeDtypeStruct(s, F32) for s in outs],
        scratch_shapes=list(scratch),
        compiler_params=pltpu.CompilerParams(vmem_limit_bytes=grant * 2**20),
    )


def swap(x, axes, n, start):
    pairs = []
    for i in range(start, n - 1, 2):
        pairs += [(i, i + 1), (i + 1, i)]
    return lax.ppermute(x, axes, pairs)


def step(flow, heat, salt):
    vmem = pltpu.VMEM
    refine = jnp.asarray(REFINE, BF16)
    refine_split = jnp.asarray(REFINE_SPLIT, BF16)
    restrict_m = jnp.asarray(RESTRICT, BF16)
    own_levels = jnp.asarray(OWN, BF16)
    all_levels = jnp.asarray(ALL, BF16)
    (a,) = call(
        turn_kernel, "hh", [(16, 2, 2, 8, 128)], [vmem((4, 2, 32, 128), F32), pltpu.SemaphoreType.DMA((2,))], grant=60
    )(flow, heat)
    g, means, planes, near_salt, far_salt = call(
        pack_kernel,
        "vv",
        [(10, 8, NX), (2, 8, NX), (4, 2, 8, NF), (3, 8, NX), (3, 8, NX)],
        [vmem((8, 4, 16, 128), F32), vmem((2, 8, NX), F32), vmem((2, 8, NX), F32)],
    )(salt, restrict_m)
    g = swap(g, "gz", 2, 0)
    near_salt = swap(near_salt, ("gx", "gy"), 128, 0)
    far_salt = swap(far_salt, ("gx", "gy"), 128, 1)
    d = lax.all_to_all(a.reshape(32, 2, 8, 128), ("gy", "gz"), 0, 0, tiled=True)
    c, near, far = call(send_kernel, "vvv", [(5, 4, 8, NX), (9, 8, NX), (9, 8, NX)])(d.reshape(16, 4, 8, 128), means, g)
    near = swap(near, ("gx", "gy"), 128, 0)
    far = swap(far, ("gx", "gy"), 128, 1)
    rims = [(12, 8, NX)] * 2
    fields = [(4, 8, 16, NX)] * 2
    msg, cp, mp, salt_mid, u, v = call(
        coarse_kernel, "vvvvvvvvvvvv", [(16, 2, 8, 128)] + fields + [(4, 2, 8, NF)] + rims, [vmem((3, 64, NF), F32)]
    )(c, near, far, near_salt, far_salt, planes, g, refine, refine_split, restrict_m, own_levels, all_levels)
    back = lax.all_to_all(msg, "gy", 0, 0, tiled=True)
    (salt_end,) = call(
        salt_kernel,
        "vvvvvvvvv",
        [(4, 16, NF)],
        [vmem((3, 64, NF), F32), vmem((3, 48, NF), F32), vmem((8, 4, 16, 128), F32)],
    )(cp, mp, salt_mid, planes, u, v, g, refine, own_levels)
    flow_end, heat_end = call(unpack_kernel, "v", [(3, 2, 32, 128), (2, 32, 128)])(back)
    return flow_end, heat_end, salt_end


def solution(mesh):
    specs = (P(None, "gz", "gy", "gx"), P("gz", "gy", "gx"), P("gz", ("gx", "gy"), None))
    return jax.shard_map(step, mesh=mesh, in_specs=specs, out_specs=specs, check_vma=False)
```

```python
import jax
import jax.numpy as jnp
import numpy as np
from jax import lax
from jax.experimental import pallas as pl
from jax.experimental.pallas import tpu as pltpu
from jax.sharding import PartitionSpec as P


F32 = jnp.float32
BF16 = jnp.bfloat16
DT = 0.1
EVEN = (-0.0390625, 0.2734375, 0.8203125, -0.0546875)
ODD = (-0.0546875, 0.8203125, 0.2734375, -0.0390625)
KINDS = (0.2, 0.2, 0.2, 0.15)
NX = 512
NF = 1024


def refine_matrix():
    matrix = np.zeros((256, 256), np.float32)
    for n in range(256):
        i = 64 + n // 2
        for k in range(4):
            matrix[i + k - (2 if n % 2 == 0 else 1), n] = (EVEN if n % 2 == 0 else ODD)[k]
    return matrix


def restrict_matrix():
    matrix = np.zeros((256, 128), np.float32)
    for n in range(256):
        matrix[n, n // 2] = 0.125
    return matrix


def level_row_matrix(levels, parts):
    rows = np.zeros((2, 16, 16), np.float64)
    for q, weights in enumerate((EVEN, ODD)):
        for i in range(16):
            for k in range(4):
                rows[q, i, (i + k - 2 + q) % 16] = weights[k]
    deep = np.zeros((len(levels), 4), np.float64)
    for n, l in enumerate(levels):
        for k in range(4):
            m = l // 2 + k - 2 + l % 2
            if 0 <= m < 4:
                deep[n, m] = (EVEN, ODD)[l % 2][k]
    whole = np.einsum("lm,qij->lqimj", deep, rows[:, :parts]).reshape(len(levels) * 2 * parts, 64)
    high = whole.astype(np.float32).astype(jnp.bfloat16).astype(np.float64)
    return np.concatenate([high, high, whole - high], axis=1).astype(np.float32)


REFINE = refine_matrix()
REFINE_SPLIT = np.concatenate([REFINE[:, 0::2], REFINE[:, 1::2]], axis=1)
RESTRICT = restrict_matrix()
OWN = np.stack([level_row_matrix(range(4 * z, 4 * z + 4), 8) for z in range(2)])
ALL = level_row_matrix(range(8), 16)


def dot(a, b):
    return jnp.dot(a, b, preferred_element_type=F32)


def split(x):
    high = x.astype(BF16)
    return high, (x - high.astype(F32)).astype(BF16)


def row(x, s):
    n = x.shape[0]
    return x if s % n == 0 else pltpu.roll(x, (-s) % n, 0)


def iota(shape, axis):
    return lax.broadcasted_iota(jnp.int32, shape, axis)


def right(x):
    n = x.shape[1] // 128
    turned = [pltpu.roll(x[:, 128 * c : 128 * c + 128], 127, 1) for c in range(n)]
    edge = iota(turned[0].shape, 1) == 127
    return jnp.concatenate([jnp.where(edge, turned[c + 1] if c < n - 1 else 0.0, turned[c]) for c in range(n)], axis=1)


def left(x):
    n = x.shape[1] // 128
    turned = [pltpu.roll(x[:, 128 * c : 128 * c + 128], 1, 1) for c in range(n)]
    edge = iota(turned[0].shape, 1) == 0
    return jnp.concatenate([jnp.where(edge, turned[c - 1] if c else 0.0, turned[c]) for c in range(n)], axis=1)


def weigh(weights, terms):
    total = None
    for w, t in zip(weights, terms):
        if t is not None:
            total = w * t if total is None else total + w * t
    return total


def refine_rows(x, keep):
    m2, m1, p1, p2 = (row(x, s)[:keep] for s in (-2, -1, 1, 2))
    x = x[:keep]
    return weigh(EVEN, (m2, m1, x, p1)), weigh(ODD, (m1, x, p1, p2))


def turn_blocks(x):
    lane = iota((8, 128), 1)
    low = lane < 64
    even = (lane // 32) % 2 == 0
    y0 = jnp.where(low, x[0], pltpu.roll(x[2], 64, 1))
    y2 = jnp.where(low, pltpu.roll(x[0], 64, 1), x[2])
    y1 = jnp.where(low, x[1], pltpu.roll(x[3], 64, 1))
    y3 = jnp.where(low, pltpu.roll(x[1], 64, 1), x[3])
    out = []
    for a, b in ((y0, y1), (y2, y3)):
        out.append(jnp.where(even, a, pltpu.roll(b, 32, 1)))
        out.append(jnp.where(even, pltpu.roll(a, 96, 1), b))
    return out


def restrict(total, matrix):
    high, low = split(total)
    parts = []
    for b in range(4):
        window = slice(256 * b, 256 * b + 256)
        parts.append(dot(high[:, window], matrix) + dot(low[:, window], matrix))
    return jnp.concatenate(parts, axis=1)


def by_levels_rows(matrix, fields):
    high, low = split(fields.reshape(64, NX))
    return dot(matrix, jnp.concatenate([high, low, high], axis=0))


def windows(x, matrix_ref, halves):
    high, low = split(x)
    parts = []
    for b in range(-1, 4):
        w = slice(max(128 * b, 0), min(128 * b + 256, NX))
        if b == -1:
            matrix = matrix_ref[128:256, :] if halves else matrix_ref[128:256, 128:256]
        elif b == 3:
            matrix = matrix_ref[0:128, :] if halves else matrix_ref[0:128, 0:128]
        else:
            matrix = matrix_ref[...]
        parts.append(dot(jnp.concatenate([high[:, w], low[:, w]], axis=1), jnp.concatenate([matrix, matrix], axis=0)))
    return parts


def refined_rows(x, matrix_ref):
    return jnp.concatenate(windows(x, matrix_ref, False), axis=1)


def heat_mean(x, keep, matrix_ref):
    sums = []
    for t in windows(x, matrix_ref, True):
        pieces = [t[keep * j : keep * j + keep, 128 * h : 128 * h + 128] for j in range(4) for h in range(2)]
        total = sum(pieces[1:], pieces[0]) + 0.5 * sum((p * p for p in pieces[1:]), pieces[0] * pieces[0])
        sums.append(pltpu.roll(total, 64, 1))
    low_half = iota((keep, 128), 1) < 64
    return 0.125 * jnp.concatenate([jnp.where(low_half, sums[c], sums[c + 1]) for c in range(4)], axis=1)


def upwind(speed, positive, below, above):
    return speed * jnp.where(positive, below, above)


def wide(ref, tile, rows):
    return jnp.concatenate([ref[tile, rows, :], ref[tile + 1, rows, :]], axis=-1)


def turn_kernel(flow_hbm, heat_hbm, a_ref, tile, sems):
    copies = [pltpu.make_async_copy(flow_hbm, tile.at[pl.ds(0, 3)], sems.at[0])]
    copies.append(pltpu.make_async_copy(heat_hbm, tile.at[3], sems.at[1]))
    for copy in copies:
        copy.start()
    for copy in copies:
        copy.wait()
    for lv in range(2):
        turned = jnp.concatenate([tile[f, lv] for f in range(4)], axis=0).T
        for j in range(16):
            piece = turned[8 * j : 8 * j + 8]
            a_ref[j, 0, lv] = piece
            a_ref[j, 1, lv] = piece


def to_sides(near_ref, far_ref, tile, up, down):
    leads = lax.rem(lax.axis_index("gy"), 2) == 0
    near_ref[tile] = jnp.where(leads, up, down)
    far_ref[tile] = jnp.where(leads, down, up)


def few_rows(a, b, c, d):
    line = iota((8, NX), 0)
    out = jnp.where(line < 2, a, pltpu.roll(b, 2, 0))
    if c is not None:
        out = jnp.where(line < 4, out, jnp.where(line == 4, c, d))
    return out


def pack_kernel(salt_ref, restrict_ref, g_ref, mean_ref, plane_ref, near_ref, far_ref, strip, up, down):
    z = lax.axis_index("gz")
    for l in range(4):
        for c in range(8):
            strip[c, l] = salt_ref[l, :, 128 * c : 128 * c + 128]
    for l in range(4):
        for q in range(2):
            for c in range(8):
                plane_ref[l, q, :, 128 * c : 128 * c + 128] = strip[c, l, pl.ds(q, 8, stride=2), :]
    totals = []
    for m in range(2):
        totals.append(sum(plane_ref[2 * m + p, q] for p in range(2) for q in range(2)))
    means = restrict(jnp.concatenate(totals, axis=0), restrict_ref[...])
    for m in range(2):
        mean_ref[m] = means[8 * m : 8 * m + 8]
        g_ref[8 + m] = means[8 * m : 8 * m + 8]
    for h in range(2):
        w = slice(512 * h, 512 * h + 512)
        for l in range(4):
            for q in range(2):
                k = 2 * l + q
                down[h, k : k + 1, :] = plane_ref[l, q, 0:1, w]
                up[h, k : k + 1, :] = plane_ref[l, q, 7:8, w]
        to_sides(near_ref, far_ref, h, up[h], down[h])
    low, high = (means[0:8], means[8:16])
    rolled = few_rows(pltpu.roll(low, 2, 0), pltpu.roll(high, 2, 0), None, None)
    to_sides(near_ref, far_ref, 2, rolled, few_rows(low, high, None, None))
    for near in range(2):
        level = jnp.where(z == 0, 3 - near, near)
        for q in range(2):
            plane = plane_ref[level, q]
            for h in range(2):
                g_ref[4 * near + 2 * q + h] = plane[:, 512 * h : 512 * h + 512]


def mean_of(mean_ref, g_ref, z, m):
    return jnp.where(z == m // 2, mean_ref[m % 2], g_ref[8 + m % 2])


def other_rows(g_ref, last):
    low, high = (g_ref[8], g_ref[9])
    if last:
        rows = [jnp.broadcast_to(g_ref[2 + h, 7:8, :], (8, NX)) for h in range(2)]
        return few_rows(pltpu.roll(low, 2, 0), pltpu.roll(high, 2, 0), rows[0], rows[1])
    rows = [jnp.broadcast_to(g_ref[h, 0:1, :], (8, NX)) for h in range(2)]
    return few_rows(low, high, rows[0], rows[1])


def send_kernel(d_ref, mean_ref, g_ref, own_ref, c_ref, near_ref, far_ref):
    z = lax.axis_index("gz")
    place = lax.axis_index("gx") * 16 + lax.axis_index("gy")
    for m in range(4):
        for b in range(4):
            tiles = turn_blocks([d_ref[4 * b + j, m] for j in range(4)])
            for f in range(4):
                c_ref[f, m, :, 128 * b : 128 * b + 128] = tiles[f]
        c_ref[4, m] = mean_of(mean_ref, g_ref, z, m)
    first = iota((8, NX), 0) < 4
    for f in range(4):
        for p in range(2):
            a = c_ref[f, 2 * p]
            b = c_ref[f, 2 * p + 1]
            down = jnp.where(first, a, pltpu.roll(b, 4, 0))
            up = jnp.where(first, pltpu.roll(a, 4, 0), b)
            to_sides(near_ref, far_ref, 2 * f + p, up, down)
    up, down = other_rows(g_ref, True), other_rows(g_ref, False)
    to_sides(near_ref, far_ref, 8, up, down)
    crossing = (place == 63) | (place == 64)
    own = jnp.where(place == 63, other_rows(own_ref, True), other_rows(own_ref, False))
    far_ref[8] = jnp.where(crossing, own, far_ref[8])


def winds(speeds):
    sizes = [DT * jnp.abs(a) for a in speeds]
    total = sizes[0] + sizes[1] + sizes[2]
    rests = {k: (1.0 - 6.0 * DT * k) - total for k in set(KINDS)}
    return [a > 0 for a in speeds], sizes, rests


def coarse_step(q, below, above, shared, diffusion, keep):
    positives, sizes, rests = shared
    x = q[:keep]
    after = (above, right(x), row(q, 1)[:keep])
    before = (below, left(x), row(q, -1)[:keep])
    around = ((after[0] + before[0]) + (after[1] + before[1])) + (after[2] + before[2])
    total = x * rests[diffusion] + (DT * diffusion) * around
    for positive, size, b, a in zip(positives, sizes, before, after):
        total = total + size * jnp.where(positive, b, a)
    return total


def salt_step(x, below, above, before, after, speeds):
    up = (above - x, after - x, right(x) - x)
    down = (x - below, x - before, x - left(x))
    spread = (up[0] - down[0]) + (up[1] - down[1]) + (up[2] - down[2])
    carried = sum(upwind(a, a > 0, d, u) for a, d, u in zip(speeds, down, up))
    return (DT * 0.05 / 0.25) * spread - (DT / 0.5) * carried


def edge_row(ref, k):
    whole = jnp.concatenate([ref[9, k : k + 1, :], ref[10, k : k + 1, :]], axis=-1)
    return jnp.broadcast_to(whole, (8, NF))


def near_edge(ref):
    whole = jnp.concatenate([ref[8, 4:5, :], ref[8, 5:6, :]], axis=-1)
    return jnp.broadcast_to(whole, (8, NF))


def levels_of(fields, f, start, parity):
    return weigh(EVEN if parity == 0 else ODD, [fields[f, start + parity + k] for k in range(4)])


def rim_of(ur_ref, dr_ref, f, m):
    first = iota((8, NX), 0) < 4
    d = dr_ref[2 * f + m // 2]
    u = ur_ref[2 * f + m // 2]
    if m % 2 == 0:
        return jnp.where(first, d, pltpu.roll(u, 4, 0))
    return jnp.where(first, pltpu.roll(d, 4, 0), u)


def coarse_kernel(
    c_ref, near_ref, far_ref, near_salt_ref, far_salt_ref, plane_ref, g_ref, refine_ref, refine_split_ref, restrict_ref, own_ref, all_ref,
    msg_ref, cp, mp, salt_mid, ur_ref, dr_ref, vel,
):
    z = lax.axis_index("gz")
    leads = lax.rem(lax.axis_index("gy"), 2) == 0
    place = lax.axis_index("gx") * 16 + lax.axis_index("gy")
    for t in range(12):
        near = near_ref[t] if t < 9 else near_salt_ref[t - 9]
        far = far_ref[t] if t < 9 else far_salt_ref[t - 9]
        ur_ref[t] = jnp.where(leads, far, near)
        dr_ref[t] = jnp.where(leads, near, far)
    zero = jnp.zeros((16, NX), F32)
    for f in range(4):
        for k in (0, 1, 6, 7):
            cp[f, k] = zero
            mp[f, k] = zero
        for m in range(4):
            cp[f, m + 2, 0:8, :] = c_ref[f, m]
            cp[f, m + 2, 8:16, :] = rim_of(ur_ref, dr_ref, f, m)
    own_matrix = own_ref[z]
    heat = by_levels_rows(all_ref[...], cp[3, 2:6])
    winding = [by_levels_rows(own_matrix, cp[f, 2:6]) for f in range(3)]
    rows16 = iota((16, NX), 0)
    inside = ((rows16 < 8) | (rows16 >= 12) | (place != 127)) & ((rows16 < 12) | (place != 0))
    two = iota((8, NX), 0) < 2
    for m in range(4):
        shared = winds([cp[f, m + 2] for f in range(3)])
        for f in (3, 1, 2, 0):
            mid = coarse_step(cp[f, m + 2], cp[f, m + 1], cp[f, m + 3], shared, KINDS[f], 16)
            if f == 0:
                own_level = z == m // 2
                below = jnp.where(own_level, dr_ref[11], dr_ref[8])
                above = jnp.where(own_level, ur_ref[11], ur_ref[8])
                if m % 2 == 1:
                    below = pltpu.roll(below, 6, 0)
                    above = pltpu.roll(above, 4, 0)
                else:
                    above = pltpu.roll(above, 6, 0)
                salt_mean = jnp.concatenate([c_ref[4, m], jnp.where(two, below, above)], axis=0)
                buoyancy = heat_mean(heat[64 * m : 64 * m + 64], 16, refine_split_ref) - 0.8 * salt_mean
                mid = mid + DT * buoyancy
            mp[f, m + 2] = jnp.where(inside, mid, 0.0)
        if m < 3:
            vel[m] = refined_rows(winding[m], refine_ref)
    heat = by_levels_rows(own_matrix, mp[3, 2:6])
    line = iota((8, NF), 0)
    totals = []
    heats = []
    for m in range(2):
        heats.append(heat_mean(heat[32 * m : 32 * m + 32], 8, refine_split_ref))
        total = None
        for p in range(2):
            l = 2 * m + p
            own = [plane_ref[l, q] for q in range(2)]
            following = jnp.where(line == 7, edge_row(dr_ref, 2 * l), pltpu.roll(own[0], 7, 0))
            preceding = jnp.where(line == 0, edge_row(ur_ref, 2 * l + 1), pltpu.roll(own[1], 1, 0))
            around = ((preceding, own[1]), (own[0], following))
            for q in range(2):
                near = wide(g_ref, 2 * q, slice(0, 8))
                below = jnp.where(z == 1, near, 0.0) if l == 0 else plane_ref[l - 1, q]
                above = jnp.where(z == 0, near, 0.0) if l == 3 else plane_ref[l + 1, q]
                speeds = [vel[f, 16 * l + 8 * q : 16 * l + 8 * q + 8, :] for f in (0, 2, 1)]
                x = own[q]
                mid = x + salt_step(x, below, above, around[q][0], around[q][1], speeds)
                salt_mid[l, q] = mid
                total = mid if total is None else total + mid
        totals.append(total)
    means = restrict(jnp.concatenate(totals, axis=0), restrict_ref[...])
    for m in range(2):
        at = 2 * z + m + 2
        shared = winds([mp[f, at, 0:8, :] for f in range(3)])
        ends = []
        for f in (1, 2, 3, 0):
            end = coarse_step(mp[f, at], mp[f, at - 1, 0:8, :], mp[f, at + 1, 0:8, :], shared, KINDS[f], 8)
            if f == 0:
                end = end + DT * (heats[m] - 0.8 * means[8 * m : 8 * m + 8])
            ends.append(0.5 * cp[f, at, 0:8, :] + 0.5 * end)
        ends = ends[3:] + ends[:3]
        for b in range(4):
            tiles = turn_blocks([ends[f][:, 128 * b : 128 * b + 128] for f in range(4)])
            for j in range(4):
                msg_ref[4 * b + j, m] = tiles[j]


def salt_kernel(
    cp, mv, salt_mid_ref, plane_ref, ur_ref, dr_ref, g_ref, refine_ref, own_ref, out_ref, vel, near_vel, strip,
):
    z = lax.axis_index("gz")
    place = lax.axis_index("gx") * 16 + lax.axis_index("gy")
    top = iota((8, NX), 0) == 0
    for f in range(3):
        rims = []
        for m in range(2):
            for p in range(2):
                even, odd = refine_rows(levels_of(cp, f, 2 * z + m, p), 16)
                rims.append(jnp.where(top, even[8:], odd[8:]))
        weights = [jnp.where(z == 0, EVEN[k], ODD[k]) for k in range(4)]
        rims.extend(refine_rows(weigh(weights, [cp[f, 2 + k] for k in range(4)]), 8))
        near_vel[f] = refined_rows(jnp.concatenate(rims, axis=0), refine_ref)
    for f in range(3):
        vel[f] = refined_rows(by_levels_rows(own_ref[z], mv[f, 2:6]), refine_ref)
    line = iota((8, NF), 0)
    rim = [jnp.where(line == 0, edge_row(dr_ref, 2 * l), edge_row(ur_ref, 2 * l + 1)) for l in range(4)]
    near_rim = jnp.where(line == 0, near_edge(dr_ref), near_edge(ur_ref))
    bottom = jnp.where(z == 1, near_rim, 0.0)
    roof = jnp.where(z == 0, near_rim, 0.0)
    alive = ((line != 0) | (place != 127)) & ((line != 7) | (place != 0))
    rim_mid = []
    for l in range(4):
        before = jnp.where(line == 0, pltpu.roll(plane_ref[l, 1], 1, 0), edge_row(ur_ref, 2 * l))
        after = jnp.where(line == 0, edge_row(dr_ref, 2 * l + 1), pltpu.roll(plane_ref[l, 0], 7, 0))
        speeds = [near_vel[f, 8 * l : 8 * l + 8, :] for f in (0, 2, 1)]
        below = bottom if l == 0 else rim[l - 1]
        above = roof if l == 3 else rim[l + 1]
        mid = rim[l] + salt_step(rim[l], below, above, before, after, speeds)
        rim_mid.append(jnp.where(alive, mid, 0.0))
    near = [wide(g_ref, 2 * q, slice(0, 8)) for q in range(2)]
    before = jnp.where(line == 0, near_edge(ur_ref), pltpu.roll(near[1], 1, 0))
    after = jnp.where(line == 7, near_edge(dr_ref), pltpu.roll(near[0], 7, 0))
    around = ((before, near[1]), (near[0], after))
    near_mid = []
    for q in range(2):
        far = wide(g_ref, 4 + 2 * q, slice(0, 8))
        below = jnp.where(z == 0, plane_ref[3, q], far)
        above = jnp.where(z == 0, far, plane_ref[0, q])
        speeds = [near_vel[f, 32 + 8 * q : 40 + 8 * q, :] for f in (0, 2, 1)]
        near_mid.append(near[q] + salt_step(near[q], below, above, around[q][0], around[q][1], speeds))
    for l in range(4):
        pair = [salt_mid_ref[l, q] for q in range(2)]
        before = pltpu.roll(jnp.where(line == 7, rim_mid[l], pair[1]), 1, 0)
        after = pltpu.roll(jnp.where(line == 0, rim_mid[l], pair[0]), 7, 0)
        around = ((before, pair[1]), (pair[0], after))
        for q in range(2):
            speeds = [vel[f, 16 * l + 8 * q : 16 * l + 8 * q + 8, :] for f in (0, 2, 1)]
            below = jnp.where(z == 1, near_mid[q], 0.0) if l == 0 else salt_mid_ref[l - 1, q]
            above = jnp.where(z == 0, near_mid[q], 0.0) if l == 3 else salt_mid_ref[l + 1, q]
            x = pair[q]
            step = salt_step(x, below, above, around[q][0], around[q][1], speeds)
            end = 0.5 * plane_ref[l, q] + 0.5 * (x + step)
            for c in range(8):
                strip[c, l, pl.ds(q, 8, stride=2), :] = end[:, 128 * c : 128 * c + 128]
        for c in range(8):
            out_ref[l, :, 128 * c : 128 * c + 128] = strip[c, l]


def unpack_kernel(x_ref, flow_ref, heat_ref):
    for lv in range(2):
        turned = jnp.concatenate([x_ref[j, lv] for j in range(16)], axis=0).T
        for f in range(3):
            flow_ref[f, lv] = turned[32 * f : 32 * f + 32]
        heat_ref[lv] = turned[96:128]


SPACES = {"h": pl.BlockSpec(memory_space=pltpu.HBM), "v": pl.BlockSpec(memory_space=pltpu.VMEM)}


def call(kernel, ins, outs, scratch=(), grant=16):
    return pl.pallas_call(
        kernel,
        in_specs=[SPACES[letter] for letter in ins],
        out_specs=[SPACES["v"] for _ in outs],
        out_shape=[jax.ShapeDtypeStruct(s, F32) for s in outs],
        scratch_shapes=list(scratch),
        compiler_params=pltpu.CompilerParams(vmem_limit_bytes=grant * 2**20),
    )


def swap(x, axes, n, start):
    pairs = []
    for i in range(start, n - 1, 2):
        pairs += [(i, i + 1), (i + 1, i)]
    return lax.ppermute(x, axes, pairs)


def beside(crossing):
    pairs = []
    for r in range(1, 127, 2):
        for z in range(2):
            other = 1 - z if r in crossing else z
            pairs += [(2 * r + z, 2 * r + 2 + other), (2 * r + 2 + other, 2 * r + z)]
    return pairs


def step(flow, heat, salt):
    vmem = pltpu.VMEM
    refine = jnp.asarray(REFINE, BF16)
    refine_split = jnp.asarray(REFINE_SPLIT, BF16)
    restrict_m = jnp.asarray(RESTRICT, BF16)
    own_levels = jnp.asarray(OWN, BF16)
    all_levels = jnp.asarray(ALL, BF16)
    (a,) = call(
        turn_kernel, "hh", [(16, 2, 2, 8, 128)], [vmem((4, 2, 32, 128), F32), pltpu.SemaphoreType.DMA((2,))], grant=60
    )(flow, heat)
    g, means, planes, near_salt, far_salt = call(
        pack_kernel,
        "vv",
        [(10, 8, NX), (2, 8, NX), (4, 2, 8, NF), (3, 8, NX), (3, 8, NX)],
        [vmem((8, 4, 16, 128), F32), vmem((2, 8, NX), F32), vmem((2, 8, NX), F32)],
    )(salt, restrict_m)
    own = g
    g = swap(g, "gz", 2, 0)
    near_salt = swap(near_salt, ("gx", "gy"), 128, 0)
    far_salt = swap(far_salt, ("gx", "gy"), 128, 1)
    d = lax.all_to_all(a.reshape(32, 2, 8, 128), ("gy", "gz"), 0, 0, tiled=True)
    c, near, far = call(send_kernel, "vvvv", [(5, 4, 8, NX), (9, 8, NX), (9, 8, NX)])(
        d.reshape(16, 4, 8, 128), means, g, own
    )
    near = swap(near, ("gx", "gy"), 128, 0)
    far = lax.ppermute(far, ("gx", "gy", "gz"), beside((63,)))
    rims = [(12, 8, NX)] * 2
    fields = [(4, 8, 16, NX)] * 2
    msg, cp, mp, salt_mid, u, v = call(
        coarse_kernel, "vvvvvvvvvvvv", [(16, 2, 8, 128)] + fields + [(4, 2, 8, NF)] + rims, [vmem((3, 64, NF), F32)]
    )(c, near, far, near_salt, far_salt, planes, g, refine, refine_split, restrict_m, own_levels, all_levels)
    back = lax.all_to_all(msg, "gy", 0, 0, tiled=True)
    (salt_end,) = call(
        salt_kernel,
        "vvvvvvvvv",
        [(4, 16, NF)],
        [vmem((3, 64, NF), F32), vmem((3, 48, NF), F32), vmem((8, 4, 16, 128), F32)],
    )(cp, mp, salt_mid, planes, u, v, g, refine, own_levels)
    flow_end, heat_end = call(unpack_kernel, "v", [(3, 2, 32, 128), (2, 32, 128)])(back)
    return flow_end, heat_end, salt_end


def solution(mesh):
    specs = (P(None, "gz", "gy", "gx"), P("gz", "gy", "gx"), P("gz", ("gx", "gy"), None))
    return jax.shard_map(step, mesh=mesh, in_specs=specs, out_specs=specs, check_vma=False)
```
